512 devices in a mesh: curve: 512 (over x, y, z, core).
Axes of the slice: x: 4, y: 8, z: 8, core: 2. Of those that a mesh axis runs over, the one named last changes fastest.
Arguments:
- vectors: bfloat16 [524288, 128], P('curve'), may hold values from -6 to 6
- near_self: bfloat16 [524288, 512], P('curve'), may hold values from -0.15625 to 0.15625
- near_next: bfloat16 [524288, 512], P('curve'), may hold values from -0.15625 to 0.15625
- leaf_basis: bfloat16 [524288, 256], P('curve'), may hold values from -0.25 to 0.25
- transfer_one: bfloat16 [262144, 256], P('curve'), may hold values from -0.25 to 0.25
- transfer_two: bfloat16 [65536, 256], P('curve'), may hold values from -0.25 to 0.25
- coupling_zero: bfloat16 [262144, 3, 256], P('curve'), may hold values from -0.21875 to 0.21875
- coupling_one: bfloat16 [65536, 3, 256], P('curve'), may hold values from -0.21875 to 0.21875
- coupling_two: bfloat16 [16384, 3, 256], P('curve'), may hold values from -0.21875 to 0.21875
- list_zero: int32 [1024, 3], P('curve'), may hold values from 0 to 1023, as said below
- list_one: int32 [256, 3], replicated, may hold values from 0 to 255, as said below
- list_two: int32 [64, 3], replicated, may hold values from 0 to 63, as said below
Outputs:
- product: bfloat16 [524288, 128], P('curve')
The draws below stay inside these ranges and needn't reach their ends.
Inputs may be any that keep to these rules, and one draw needn't show every extreme that they name: `list_zero`: row c holds 3 different entries (c + d) mod 1024, each d one of -3, -2, 2, 3. `list_one`: row p holds 3 entries (p + d) mod 256 for different d among -3, -2, 2, 3. `list_two`: row q holds 3 entries (q + d) mod 64 for different d among -3, -2, 2, 3.
All inputs are finite; a program needn't handle non-finite values.
Results may differ from the reference program's by a relative error of at most 0.014.
Values may be sent and summed in bfloat16 or wider, within the bound.
No kernel may reach another device: no remote copies, remote signals or barrier semaphores. Data moves between devices by JAX's collectives and lax.ppermute only.
A program may use at most 64 MiB of HBM per device.

```python
import jax
import jax.numpy as jnp

M = 512
K = 256
R = 128
SLOTS = 3
LEAVES = 1024
CLUSTERS_ONE = 256
CLUSTERS_TWO = 64
ORDER = 524288
N_CURVE = 512


def listed_partners(key, clusters):
    offsets = jnp.array([-3, -2, 2, 3], jnp.int32)
    ranking = jax.random.randint(key, (clusters, 4), 0, 1 << 20) * 4 + jnp.arange(4, dtype=jnp.int32)[None, :]
    picked = jnp.argsort(ranking, axis=1)[:, :SLOTS]
    cluster_ids = jnp.arange(clusters, dtype=jnp.int32)[:, None]
    return ((cluster_ids + offsets[picked]) % clusters).astype(jnp.int32)


def draw_list_zero(key, part):
    return listed_partners(jax.random.fold_in(key, 101), LEAVES)


def draw_list_one(key, part):
    return listed_partners(jax.random.fold_in(key, 202), CLUSTERS_ONE)


def draw_list_two(key, part):
    return listed_partners(jax.random.fold_in(key, 303), CLUSTERS_TWO)


def level_of(rng, extent, cuts, least, high):
    def one(position, shards_of):
        heights = jax.random.uniform(jax.random.fold_in(jax.random.fold_in(rng, 6), position), (shards_of,), jnp.float32, least / len(cuts), high / len(cuts))
        return jnp.repeat(jnp.exp(heights), extent[position] // shards_of).reshape((-1,) + (1,) * (len(extent) - position - 1))

    factor_of = one(*cuts[0])
    for cut in cuts[1:]:
        factor_of = factor_of * one(*cut)
    return factor_of


def centred(own_key, dims, scale, bound, pieces=(), kind=jnp.bfloat16):
    result = scale * jax.random.normal(own_key, dims, jnp.float32)
    if pieces:
        result = result * level_of(own_key, dims, pieces, -0.22, 0.18)
    return jnp.clip(result, -bound, bound).astype(kind)


def setup_inputs(seed: int = 0) -> dict:
    streams_of = jax.random.split(jax.random.key(seed), 13)
    return {
        "vectors": centred(streams_of[0], (ORDER, R), 1.0, 6.0, ((0, 512),)),
        "near_self": centred(streams_of[1], (ORDER, M), (3 * M) ** -0.5, 0.15625, ((0, 512),)),
        "near_next": centred(streams_of[2], (ORDER, M), (3 * M) ** -0.5, 0.15625, ((0, 512),)),
        "leaf_basis": centred(streams_of[3], (ORDER, K), M ** -0.5, 0.25, ((0, 512),)),
        "transfer_one": centred(streams_of[4], (LEAVES * K, K), (2 * K) ** -0.5, 0.25, ((0, 512),)),
        "transfer_two": centred(streams_of[5], (CLUSTERS_ONE * K, K), (2 * K) ** -0.5, 0.25, ((0, 512),)),
        "coupling_zero": centred(streams_of[6], (LEAVES * K, SLOTS, K), (SLOTS * K) ** -0.5, 0.21875, ((0, 512),)),
        "coupling_one": centred(streams_of[7], (CLUSTERS_ONE * K, SLOTS, K), (SLOTS * K) ** -0.5, 0.21875, ((0, 512),)),
        "coupling_two": centred(streams_of[8], (CLUSTERS_TWO * K, SLOTS, K), (SLOTS * K) ** -0.5, 0.21875, ((0, 512),)),
        "list_zero": draw_list_zero(jax.random.fold_in(streams_of[12], 71), 0),
        "list_one": draw_list_one(jax.random.fold_in(streams_of[12], 71), 0),
        "list_two": draw_list_two(jax.random.fold_in(streams_of[12], 71), 0),
    }


def lift(coefficients, transfer, clusters):
    blocks = transfer.reshape(clusters, K, K).astype(jnp.float32)
    terms = jnp.einsum("cab,car->cbr", blocks, coefficients.astype(jnp.float32))
    return terms.reshape(clusters // 4, 4, K, R).sum(axis=1).astype(jnp.bfloat16)


def couple(coefficients, coupling, interaction_rows, clusters):
    blocks = coupling.reshape(clusters, K, SLOTS, K).astype(jnp.float32)
    sources = coefficients.astype(jnp.float32)[interaction_rows]
    return jnp.einsum("casb,csar->cbr", blocks, sources)


def expand(far_terms, parent_terms, transfer, clusters):
    blocks = transfer.reshape(clusters, K, K).astype(jnp.float32)
    spread = jnp.repeat(parent_terms.astype(jnp.float32), 4, axis=0)
    return (far_terms + jnp.einsum("cab,cbr->car", blocks, spread)).astype(jnp.bfloat16)


def reference(vectors, near_self, near_next, leaf_basis, transfer_one, transfer_two, coupling_zero, coupling_one, coupling_two, list_zero, list_one, list_two):
    leaf_clusters = 2 * N_CURVE
    points = vectors.reshape(leaf_clusters, M, R).astype(jnp.float32)
    basis = leaf_basis.reshape(leaf_clusters, M, K).astype(jnp.float32)
    coef_zero = jnp.einsum("cmk,cmr->ckr", basis, points).astype(jnp.bfloat16)
    coef_one = lift(coef_zero, transfer_one, leaf_clusters)
    coef_two = lift(coef_one, transfer_two, leaf_clusters // 4)
    far_zero = couple(coef_zero, coupling_zero, list_zero, leaf_clusters)
    far_one = couple(coef_one, coupling_one, list_one, leaf_clusters // 4)
    far_two = couple(coef_two, coupling_two, list_two, leaf_clusters // 16)
    expansion_two = far_two.astype(jnp.bfloat16)
    expansion_first_level = expand(far_one, expansion_two, transfer_two, leaf_clusters // 4)
    expansion_zero = expand(far_zero, expansion_first_level, transfer_one, leaf_clusters)
    far_field = jnp.einsum("cmk,ckr->cmr", basis, expansion_zero.astype(jnp.float32))
    self_blocks = near_self.reshape(leaf_clusters, M, M).astype(jnp.float32)
    next_blocks = near_next.reshape(leaf_clusters, M, M).astype(jnp.float32)
    near_field = jnp.einsum("cmn,cnr->cmr", self_blocks, points)
    near_field = near_field + jnp.einsum("cmn,cnr->cmr", next_blocks, jnp.roll(points, -1, axis=0))
    near_field = near_field + jnp.roll(jnp.einsum("cmn,cmr->cnr", next_blocks, points), 1, axis=0)
    return (near_field + far_field).astype(jnp.bfloat16).reshape(leaf_clusters * M, R)
```

```python
import jax
import jax.numpy as jnp
from jax import lax
from jax.sharding import PartitionSpec as P

F32 = jnp.float32
BF16 = jnp.bfloat16


def route(value, source_of):
    size = lax.axis_size("curve")
    return lax.ppermute(value, "curve", [(source_of(i) % size, i) for i in range(size)])


def core_swap(value):
    return route(value, lambda i: i ^ 1)


def chip_swap(value):
    return route(value, lambda i: i + 1 if i & 1 else i - 1)


def far_route(value, chips):
    return route(value, lambda i: i + 2 * chips if i & 1 else i - 2 * chips)


def chip_groups(size):
    return [[8 * g + 2 * i + j for i in range(4)] for g in range(size // 8) for j in range(2)]


def dot_tn(a, b):
    return lax.dot_general(a, b, (((0,), (0,)), ((), ())), preferred_element_type=F32)


def dot_nn(a, b):
    return lax.dot_general(a, b, (((1,), (0,)), ((), ())), preferred_element_type=F32)


def slots_of(row, own, clusters, core):
    distance = (row - own) % clusters
    near = jnp.where(core == 0, -2, 2) % clusters
    far = jnp.where(core == 0, -3, 3) % clusters
    return distance == near, distance == far


def pick(masks, near, far):
    m, n = masks
    zero = jnp.zeros((), near.dtype)
    return jnp.where(
        m[:, None, None], near[None], jnp.where(n[:, None, None], far[None], zero)
    )


def couple(weights, chosen):
    total = dot_tn(weights[0], chosen[0])
    for s in range(1, weights.shape[0]):
        total = total + dot_tn(weights[s], chosen[s])
    return total


def per_device(
    vectors,
    near_self,
    near_next,
    leaf_basis,
    transfer_one,
    transfer_two,
    coupling_zero,
    coupling_one,
    coupling_two,
    list_zero,
    list_one,
    list_two,
):
    size = lax.axis_size("curve")
    device = lax.axis_index("curve")
    core = device & 1
    rank = leaf_basis.shape[1]
    columns = vectors.shape[1]
    points = near_self.shape[1]
    x = vectors.reshape(2, points, columns)
    basis = leaf_basis.reshape(2, points, rank)
    e1 = transfer_one.reshape(2, rank, rank)
    c0 = jnp.transpose(coupling_zero, (1, 0, 2))
    c1 = jnp.transpose(coupling_one, (1, 0, 2))
    c2 = jnp.transpose(coupling_two, (1, 0, 2))

    def columns_of(w):
        return jnp.concatenate([w[..., :128].reshape(-1, 128), w[..., 128:].reshape(-1, 128)], 0)

    def back(rows, shape):
        half = rows.shape[0] // 2
        return jnp.concatenate(
            [rows[:half].reshape(shape[:-1] + (128,)), rows[half:].reshape(shape[:-1] + (128,))], -1
        )

    coef = jnp.stack([dot_tn(basis[i], x[i]).astype(BF16) for i in range(2)], 0)
    part_one = (dot_tn(e1[0], coef[0]) + dot_tn(e1[1], coef[1])).astype(BF16)

    pieces = [coef.reshape(-1, columns), part_one, columns_of(transfer_two), columns_of(c1), columns_of(c2)]
    sizes = [p.shape[0] for p in pieces]
    got = core_swap(jnp.concatenate(pieces, 0))
    cuts = []
    at = 0
    for n in sizes:
        cuts.append(got[at : at + n])
        at += n
    partner_coef = cuts[0].reshape(coef.shape)
    first = core == 0

    def in_order(mine, other, axis):
        return jnp.concatenate(
            [jnp.where(first, mine, other), jnp.where(first, other, mine)], axis
        )

    coef_one = (part_one.astype(F32) + cuts[1].astype(F32)).astype(BF16)
    e2 = in_order(transfer_two, back(cuts[2], transfer_two.shape), 0)
    c1 = in_order(c1, back(cuts[3], c1.shape), 1)
    c2 = in_order(c2, back(cuts[4], c2.shape), 1)

    part_two = dot_tn(e2, coef_one).astype(BF16)
    shares = lax.all_to_all(
        part_two.reshape(4, rank // 4, columns), "curve", 0, 0, axis_index_groups=chip_groups(size)
    )
    coef_two = shares.astype(F32).sum(0).astype(BF16)

    two_far = far_route(coef_two, 12)
    two_near = far_route(coef_two, 8)
    one_near = far_route(coef_one, 2)
    one_far = far_route(coef_one, 3)

    outgoing = dot_tn(near_next[points:], x[1]).astype(BF16)
    ahead = x[0]
    leaves = jnp.concatenate(
        [
            jnp.where(first, coef[0], partner_coef[1]),
            jnp.where(first, coef[1], coef[0]),
            jnp.where(first, partner_coef[0], coef[1]),
            jnp.where(first, ahead, outgoing),
        ],
        0,
    )
    crossed = chip_swap(leaves)
    b = crossed[: 3 * rank].reshape(3, rank, columns)
    cross_near = crossed[3 * rank :]

    clusters_two = size // 8
    row_two = lax.dynamic_slice_in_dim(list_two, device // 8, 1, 0)[0]
    masks_two = slots_of(row_two, device // 8, clusters_two, core)
    far_two = couple(c2, pick(masks_two, two_near, two_far)).astype(BF16)
    gathered = lax.all_to_all(
        jnp.broadcast_to(far_two[None], (4,) + far_two.shape),
        "curve",
        0,
        0,
        axis_index_groups=chip_groups(size),
    )
    expansion_two = gathered.astype(F32).sum(0).astype(BF16)

    clusters_one = size // 2
    row_one = lax.dynamic_slice_in_dim(list_one, device // 2, 1, 0)[0]
    masks_one = slots_of(row_one, device // 2, clusters_one, core)
    far_one = couple(c1, pick(masks_one, one_near, one_far))
    share_one = (far_one + dot_nn(e2, expansion_two)).astype(BF16)

    last = core_swap(
        jnp.concatenate(
            [share_one, jnp.where(first, b[2], b[0]), jnp.where(first, outgoing, ahead)], 0
        )
    )
    expansion_one = (share_one.astype(F32) + last[:rank].astype(F32)).astype(BF16)
    window = jnp.concatenate([b, partner_coef, last[None, rank : 2 * rank]], 0)
    pair_near = last[2 * rank :]

    leaf = 2 * device + jnp.arange(2, dtype=jnp.int32)
    distance = (list_zero - leaf[:, None]) % (2 * size)
    code = jnp.where(distance == 2, 2, jnp.where(distance == 3, 3, jnp.where(distance == 2 * size - 2, 1, 0)))
    table = jnp.array(
        [[[0, 1, 3, 4], [1, 2, 4, 5]], [[5, 3, 0, 1], [3, 4, 1, 2]]], jnp.int32
    )
    places = table[core]
    index = jnp.take_along_axis(places, code, axis=1)
    chosen = window[index]

    incoming = jnp.where(first, cross_near, pair_near)
    following = jnp.where(first, pair_near, cross_near)
    out = []
    for i in range(2):
        far_zero = couple(c0[:, i * rank : (i + 1) * rank], chosen[i])
        expansion_zero = (far_zero + dot_nn(e1[i], expansion_one)).astype(BF16)
        near = dot_nn(near_self[i * points : (i + 1) * points], x[i])
        near = near + dot_nn(near_next[i * points : (i + 1) * points], x[1] if i == 0 else following)
        if i == 0:
            near = near + incoming.astype(F32)
        else:
            near = near + dot_tn(near_next[:points], x[0])
        out.append((near + dot_nn(basis[i], expansion_zero)).astype(BF16))
    return jnp.concatenate(out, 0)


def solution(mesh):
    rows = P("curve", None)
    cube = P("curve", None, None)
    return jax.shard_map(
        per_device,
        mesh=mesh,
        in_specs=(rows, rows, rows, rows, rows, rows, cube, cube, cube, rows, P(), P()),
        out_specs=rows,
        check_vma=False,
    )
```

```python
import functools

import jax
import jax.numpy as jnp
from jax import lax
from jax.experimental import pallas as pl
from jax.experimental.pallas import tpu as pltpu
from jax.sharding import PartitionSpec as P


F32 = jnp.float32
BF16 = jnp.bfloat16
I32 = jnp.int32


def route(value, source_of):
    size = lax.axis_size("curve")
    return lax.ppermute(value, "curve", [(source_of(i) % size, i) for i in range(size)])


def core_swap(value):
    return route(value, lambda i: i ^ 1)


def chip_swap(value):
    return route(value, lambda i: i + 1 if i & 1 else i - 1)


def far_route(value, chips):
    return route(value, lambda i: i + 2 * chips if i & 1 else i - 2 * chips)


def third_cluster(value):
    def source_of(i):
        turned = i ^ 4
        return turned + 24 if i & 1 else turned - 24

    return route(value, source_of)


def chip_groups(size):
    return [[8 * g + 2 * i + j for i in range(4)] for g in range(size // 8) for j in range(2)]


def cluster_groups(size):
    return [[8 * g + i for i in range(8)] for g in range(size // 8)]


def nn(a, b):
    return lax.dot_general(a, b, (((1,), (0,)), ((), ())), preferred_element_type=F32)


def nt(a, b):
    return lax.dot_general(a, b, (((1,), (1,)), ((), ())), preferred_element_type=F32)


def call(body, outs, flops, *args, far=False, scratch=(), grant=8):
    spec = pl.BlockSpec(memory_space=pltpu.VMEM)
    moved = sum(a.size * a.dtype.itemsize for a in args)
    if far:
        args = [pltpu.with_memory_space_constraint(a, pltpu.HBM) for a in args]
    return pl.pallas_call(
        body,
        out_shape=[jax.ShapeDtypeStruct(s, t) for s, t in outs],
        in_specs=[pl.BlockSpec(memory_space=pltpu.HBM) if far else spec] * len(args),
        out_specs=[spec] * len(outs),
        scratch_shapes=list(scratch),
        compiler_params=pltpu.CompilerParams(vmem_limit_bytes=grant << 20),
        cost_estimate=pl.CostEstimate(flops=flops, bytes_accessed=moved, transcendentals=0),
    )(*args)


def picked_row(table, row):
    lanes = lax.broadcasted_iota(I32, table.shape, 1)
    return jnp.sum(jnp.where(lanes == row, table, 0), axis=1, keepdims=True)


def offset_mask(entry, own, offset, clusters):
    wanted = lax.rem(own + offset + clusters, clusters)
    return jnp.where(entry == wanted, 1.0, 0.0).astype(F32)


def spread_body(table_ref, coupling_ref, out_ref):
    device = lax.axis_index("curve")
    clusters = table_ref.shape[1]
    own = device // 8
    row = picked_row(table_ref[...], own)
    for core, offsets in enumerate(((-2, -3), (2, 3))):
        for n, offset in enumerate(offsets):
            total = None
            for s in range(3):
                mask = offset_mask(row[s : s + 1], own, offset, clusters)
                term = coupling_ref[s].astype(F32) * mask
                total = term if total is None else total + term
            value = total.astype(BF16)
            for chip in range(4):
                out_ref[2 * chip + core, n] = value


def first_body(
    points, rank, basis_hbm, x_hbm, e1_hbm, next_hbm, e2_hbm, c1_hbm, pack_ref, cross_ref,
    basis_ref, x_ref, e1_ref, next_ref, sems,
):
    core = lax.axis_index("curve") & 1
    copies = []
    for i in range(2):
        rows = pl.ds(i * points, points)
        copies.append((x_hbm.at[rows], x_ref.at[rows]))
        copies.append((basis_hbm.at[rows], basis_ref.at[rows]))
    copies.append((e1_hbm, e1_ref))
    copies.append((next_hbm.at[pl.ds(points, points)], next_ref))
    copies.append((e2_hbm, pack_ref.at[pl.ds(640, 128)]))
    for s in range(3):
        copies.append((c1_hbm.at[s], pack_ref.at[pl.ds(768 + 128 * s, 128)]))
    moves = [pltpu.make_async_copy(a, b, sems.at[n]) for n, (a, b) in enumerate(copies)]
    for move in moves:
        move.start()
    coefs = []
    for i in range(2):
        moves[2 * i].wait()
        turned = x_ref[i * points : (i + 1) * points].T
        moves[2 * i + 1].wait()
        coef = nn(turned, basis_ref[i * points : (i + 1) * points]).astype(BF16)
        pack_ref[128 * i : 128 * (i + 1)] = coef
        coefs.append(coef)
    moves[4].wait()
    part = nn(coefs[0], e1_ref[0:rank]) + nn(coefs[1], e1_ref[rank : 2 * rank])
    pack_ref[256:384] = part.astype(BF16)
    moves[5].wait()
    outgoing = nn(turned, next_ref[...]).astype(BF16)
    first = core == 0
    for h in range(2):
        sent = outgoing[:, 256 * h : 256 * (h + 1)]
        low = x_ref[128 * h : 128 * (h + 1)]
        high = x_ref[256 + 128 * h : 256 + 128 * (h + 1)]
        ahead = jnp.concatenate([low, high], 1)
        pack_ref[384 + 128 * h : 512 + 128 * h] = jnp.where(first, sent, ahead)
        cross_ref[128 * h : 128 * (h + 1)] = jnp.where(first, ahead, sent)
    for move in moves[6:]:
        move.wait()


def second_body(pack_ref, got_ref, one_ref, two_ref):
    first = (lax.axis_index("curve") & 1) == 0
    one = (pack_ref[256:384].astype(F32) + got_ref[256:384].astype(F32)).astype(BF16)
    one_ref[...] = one
    mine = pack_ref[640:768]
    other = got_ref[640:768]
    top = jnp.where(first, mine, other)
    bottom = jnp.where(first, other, mine)
    two_ref[...] = (nn(one[:, 0:128], top) + nn(one[:, 128:256], bottom)).astype(BF16)


def cross_body(pack_ref, got_ref, near_ref, out_ref):
    first = (lax.axis_index("curve") & 1) == 0
    out_ref[0:128] = jnp.where(first, pack_ref[0:128], got_ref[128:256])
    out_ref[128:256] = jnp.where(first, pack_ref[128:256], pack_ref[0:128])
    out_ref[256:384] = jnp.where(first, got_ref[0:128], pack_ref[128:256])
    out_ref[384:640] = near_ref[...]


def near_body(points, self_ref, next_ref, x_ref, out_ref):
    x0 = x_ref[0:points]
    x1 = x_ref[points : 2 * points]
    out_ref[0:points] = nn(self_ref[0:points], x0) + nn(next_ref[0:points], x1)
    inner = nn(x0.T, next_ref[0:points])
    out_ref[points : 2 * points] = nn(self_ref[points : 2 * points], x1) + inner.T


def couple_two_body(near_ref, far_ref, weights_ref, out_ref):
    near = near_ref[...]
    far = far_ref[...]
    total = None
    for m in range(8):
        piece = nn(near[:, 32 * m : 32 * (m + 1)], weights_ref[m, 0])
        piece = piece + nn(far[:, 32 * m : 32 * (m + 1)], weights_ref[m, 1])
        total = piece if total is None else total + piece
    value = total.astype(BF16)
    for i in range(4):
        out_ref[i] = value


def gather_body(
    points,
    rank,
    table_ref,
    leaf_ref,
    pack_ref,
    got_ref,
    near_ref,
    far_ref,
    cross_ref,
    c0_ref,
    part_ref,
    next_ref,
    one_ref,
    zero_ref,
    weight_ref,
    field_ref,
    send_ref,
):
    device = lax.axis_index("curve")
    core = device & 1
    first = core == 0
    clusters = table_ref.shape[1]
    own = device // 2
    sign = jnp.where(first, -1, 1)
    row = picked_row(table_ref[...], own)
    near = near_ref[...].astype(F32)
    far = far_ref[...].astype(F32)
    total = None
    for s in range(3):
        entry = row[s : s + 1]
        chosen = near * offset_mask(entry, own, 2 * sign, clusters)
        chosen = chosen + far * offset_mask(entry, own, 3 * sign, clusters)
        chosen = chosen.astype(BF16)
        mine = pack_ref[768 + 128 * s : 896 + 128 * s]
        other = got_ref[768 + 128 * s : 896 + 128 * s]
        term = nn(chosen[:, 0:128], jnp.where(first, mine, other))
        term = term + nn(chosen[:, 128:256], jnp.where(first, other, mine))
        total = term if total is None else total + term
    one_ref[...] = total

    leaves = clusters * 4
    cross = [cross_ref[128 * n : 128 * (n + 1)].astype(F32) for n in range(3)]
    partner = [got_ref[128 * n : 128 * (n + 1)].astype(F32) for n in range(2)]
    send_ref[...] = jnp.where(first, cross_ref[256:384], cross_ref[0:128])

    def either(a, b):
        return jnp.where(first, a, b)

    nothing = jnp.zeros_like(cross[0])
    tables = (
        (
            (-3, either(cross[0], nothing)),
            (-2, either(cross[1], partner[0])),
            (2, either(partner[0], cross[0])),
            (3, either(partner[1], cross[1])),
        ),
        (
            (-3, either(cross[1], partner[0])),
            (-2, either(cross[2], partner[1])),
            (2, either(partner[1], cross[1])),
            (3, either(nothing, cross[2])),
        ),
    )
    weight = None
    for i in range(2):
        leaf = 2 * device + i
        total = None
        for s in range(3):
            entry = leaf_ref[i : i + 1, s : s + 1]
            chosen = None
            for offset, value in tables[i]:
                term = value * offset_mask(entry, leaf, offset, leaves)
                chosen = term if chosen is None else chosen + term
            block = c0_ref[s, i * rank : (i + 1) * rank]
            term = nn(chosen.astype(BF16), block)
            total = term if total is None else total + term
            edge = offset_mask(entry, leaf, 3 if i else -3, leaves)
            edge = edge * jnp.where(core == (1 - i), 1.0, 0.0)
            term = block.astype(F32) * edge
            weight = term if weight is None else weight + term
        zero_ref[128 * i : 128 * (i + 1)] = total
    weight_ref[...] = weight.astype(BF16)

    pieces = []
    ahead = []
    for h in range(2):
        paired = got_ref[384 + 128 * h : 512 + 128 * h]
        crossed = cross_ref[384 + 128 * h : 512 + 128 * h]
        pieces.append(jnp.where(first, crossed, paired))
        ahead.append(jnp.where(first, paired, crossed))
    incoming = jnp.concatenate(pieces, 1).astype(F32).T
    following = jnp.concatenate(
        [ahead[0][:, 0:128], ahead[1][:, 0:128], ahead[0][:, 128:256], ahead[1][:, 128:256]], 0
    )
    field_ref[0:points] = part_ref[0:points] + incoming
    field_ref[points : 2 * points] = part_ref[points : 2 * points] + nn(
        next_ref[points : 2 * points], following
    )


def share_body(gathered_ref, one_ref, pack_ref, got_ref, send_ref, out_ref):
    first = (lax.axis_index("curve") & 1) == 0
    mine = pack_ref[640:768]
    other = got_ref[640:768]
    total = gathered_ref[0].astype(F32)
    for i in range(1, 4):
        total = total + gathered_ref[i].astype(F32)
    total = total.astype(BF16)
    top = nt(total, jnp.where(first, mine, other))
    bottom = nt(total, jnp.where(first, other, mine))
    out_ref[0:128] = (one_ref[...] + jnp.concatenate([top, bottom], 1)).astype(BF16)
    out_ref[128:256] = send_ref[...]


def last_body(points, rank, mine_ref, got_ref, zero_ref, weight_ref, e1_ref, basis_ref, field_ref, out_ref):
    core = lax.axis_index("curve") & 1
    one = (mine_ref[0:128].astype(F32) + got_ref[0:128].astype(F32)).astype(BF16)
    extra = nn(got_ref[128:256], weight_ref[...])
    for i in range(2):
        used = jnp.where(core == (1 - i), 1.0, 0.0)
        zero = zero_ref[128 * i : 128 * (i + 1)] + extra * used
        zero = zero + nt(one, e1_ref[i * rank : (i + 1) * rank])
        field = nt(basis_ref[i * points : (i + 1) * points], zero.astype(BF16))
        out_ref[i * points : (i + 1) * points] = (
            field_ref[i * points : (i + 1) * points] + field
        ).astype(BF16)


def local_part(
    vectors,
    near_self,
    near_next,
    leaf_basis,
    transfer_one,
    transfer_two,
    coupling_zero,
    coupling_one,
    coupling_two,
    list_zero,
    list_one,
    list_two,
):
    size = lax.axis_size("curve")
    rank = leaf_basis.shape[1]
    points = near_self.shape[1]
    c0 = jnp.transpose(coupling_zero, (1, 0, 2))
    c1 = jnp.transpose(coupling_one, (1, 0, 2))
    c2 = jnp.transpose(coupling_two, (1, 0, 2))
    table_one = list_one.T
    table_two = list_two.T

    (spread,) = call(spread_body, [((8, 2, 32, 256), BF16)], 1 << 18, table_two, c2)
    weights_two = lax.all_to_all(
        spread, "curve", 0, 0, axis_index_groups=cluster_groups(size)
    )
    pack, near_cross = call(
        functools.partial(first_body, points, rank),
        [((1152, 256), BF16), ((256, 256), BF16)],
        160 << 20,
        leaf_basis,
        vectors,
        transfer_one,
        near_next,
        transfer_two,
        c1,
        far=True,
        scratch=[
            pltpu.VMEM((2 * points, rank), BF16),
            pltpu.VMEM((2 * points, 128), BF16),
            pltpu.VMEM((2 * rank, rank), BF16),
            pltpu.VMEM((points, points), BF16),
            pltpu.SemaphoreType.DMA((10,)),
        ],
    )
    got = core_swap(pack)
    one, two = call(second_body, [((128, 256), BF16), ((128, 256), BF16)], 16 << 20, pack, got)
    two_far = third_cluster(two)
    two_near = far_route(two, 8)
    (leaves,) = call(cross_body, [((640, 256), BF16)], 1 << 18, pack, got, near_cross)
    crossed = chip_swap(leaves)
    one_near = far_route(one, 2)
    one_far = far_route(one, 3)
    (near_part,) = call(
        functools.partial(near_body, points),
        [((2 * points, 128), F32)],
        320 << 20,
        near_self,
        near_next,
        vectors,
    )
    (coupled,) = call(
        couple_two_body, [((4, 128, 256), BF16)], 32 << 20, two_near, two_far, weights_two
    )
    gathered = lax.all_to_all(coupled, "curve", 0, 0, axis_index_groups=chip_groups(size))
    far_one, far_zero, weight, field, send = call(
        functools.partial(gather_body, points, rank),
        [
            ((128, 256), F32),
            ((256, 256), F32),
            ((256, 256), BF16),
            ((2 * points, 128), F32),
            ((128, 256), BF16),
        ],
        220 << 20,
        table_one,
        list_zero,
        pack,
        got,
        one_near,
        one_far,
        crossed,
        c0,
        near_part,
        near_next,
    )
    (share,) = call(share_body, [((256, 256), BF16)], 16 << 20, gathered, far_one, pack, got, send)
    last = core_swap(share)
    (out,) = call(
        functools.partial(last_body, points, rank),
        [((2 * points, 128), BF16)],
        120 << 20,
        share,
        last,
        far_zero,
        weight,
        transfer_one,
        leaf_basis,
        field,
    )
    return out


def solution(mesh):
    rows = P("curve", None)
    cube = P("curve", None, None)
    return jax.shard_map(
        local_part,
        mesh=mesh,
        in_specs=(rows, rows, rows, rows, rows, rows, cube, cube, cube, rows, P(), P()),
        out_specs=rows,
        check_vma=False,
    )
```

```python
import functools

import jax
import jax.numpy as jnp
from jax import lax
from jax.experimental import pallas as pl
from jax.experimental.pallas import tpu as pltpu
from jax.sharding import PartitionSpec as P


F32 = jnp.float32
BF16 = jnp.bfloat16
I32 = jnp.int32


def route(value, source_of):
    size = lax.axis_size("curve")
    return lax.ppermute(value, "curve", [(source_of(i) % size, i) for i in range(size)])


def core_swap(value):
    return route(value, lambda i: i ^ 1)


def chip_swap(value):
    return route(value, lambda i: i + 1 if i & 1 else i - 1)


def far_route(value, chips):
    return route(value, lambda i: i + 2 * chips if i & 1 else i - 2 * chips)


def third_cluster(value):
    def source_of(i):
        turned = i ^ 4
        return turned + 24 if i & 1 else turned - 24

    return route(value, source_of)


def chip_groups(size):
    return [[8 * g + 2 * i + j for i in range(4)] for g in range(size // 8) for j in range(2)]


def cluster_groups(size):
    return [[8 * g + i for i in range(8)] for g in range(size // 8)]


def nn(a, b):
    return lax.dot_general(a, b, (((1,), (0,)), ((), ())), preferred_element_type=F32)


def nt(a, b):
    return lax.dot_general(a, b, (((1,), (1,)), ((), ())), preferred_element_type=F32)


def call(body, outs, flops, *args, far=(), scratch=(), grant=8):
    spec = pl.BlockSpec(memory_space=pltpu.VMEM)
    moved = sum(a.size * a.dtype.itemsize for a in args)
    args = [
        pltpu.with_memory_space_constraint(a, pltpu.HBM) if n in far else a
        for n, a in enumerate(args)
    ]
    hbm = pl.BlockSpec(memory_space=pltpu.HBM)
    return pl.pallas_call(
        body,
        out_shape=[jax.ShapeDtypeStruct(s, t) for s, t in outs],
        in_specs=[hbm if n in far else spec for n in range(len(args))],
        out_specs=[spec] * len(outs),
        scratch_shapes=list(scratch),
        compiler_params=pltpu.CompilerParams(vmem_limit_bytes=grant << 20),
        cost_estimate=pl.CostEstimate(flops=flops, bytes_accessed=moved, transcendentals=0),
    )(*args)


def picked_row(table, row):
    lanes = lax.broadcasted_iota(I32, table.shape, 1)
    return jnp.sum(jnp.where(lanes == row, table, 0), axis=1, keepdims=True)


def offset_mask(entry, own, offset, clusters):
    wanted = lax.rem(own + offset + clusters, clusters)
    return jnp.where(entry == wanted, 1.0, 0.0).astype(F32)


def spread_body(table_ref, coupling_ref, out_ref):
    device = lax.axis_index("curve")
    clusters = table_ref.shape[1]
    own = device // 8
    row = picked_row(table_ref[...], own)
    for core, offsets in enumerate(((-2, -3), (2, 3))):
        for n, offset in enumerate(offsets):
            total = None
            for s in range(3):
                mask = offset_mask(row[s : s + 1], own, offset, clusters)
                term = coupling_ref[s].astype(F32) * mask
                total = term if total is None else total + term
            value = total.astype(BF16)
            for chip in range(4):
                out_ref[2 * chip + core, n] = value


def first_body(
    points, rank, basis_hbm, x_hbm, e1_hbm, next_hbm, e2_hbm, c1_hbm, pack_ref,
    basis_ref, x_ref, e1_ref, next_ref, sems,
):
    copies = []
    for i in range(2):
        rows = pl.ds(i * points, points)
        copies.append((x_hbm.at[rows], x_ref.at[rows]))
        copies.append((basis_hbm.at[rows], basis_ref.at[rows]))
    copies.append((e1_hbm, e1_ref))
    copies.append((next_hbm.at[pl.ds(points, points)], next_ref))
    copies.append((e2_hbm, pack_ref.at[pl.ds(896, 128)]))
    for s in range(3):
        copies.append((c1_hbm.at[s], pack_ref.at[pl.ds(1024 + 128 * s, 128)]))
    moves = [pltpu.make_async_copy(a, b, sems.at[n]) for n, (a, b) in enumerate(copies)]
    for move in moves:
        move.start()
    coefs = []
    for i in range(2):
        moves[2 * i].wait()
        turned = x_ref[i * points : (i + 1) * points].T
        moves[2 * i + 1].wait()
        coef = nn(turned, basis_ref[i * points : (i + 1) * points]).astype(BF16)
        pack_ref[128 * i : 128 * (i + 1)] = coef
        coefs.append(coef)
    moves[4].wait()
    part = nn(coefs[0], e1_ref[0:rank]) + nn(coefs[1], e1_ref[rank : 2 * rank])
    pack_ref[256:384] = part.astype(BF16)
    moves[5].wait()
    outgoing = nn(turned, next_ref[...]).astype(BF16)
    for h in range(2):
        pack_ref[384 + 128 * h : 512 + 128 * h] = outgoing[:, 256 * h : 256 * (h + 1)]
        for v in range(2):
            rows = x_ref[256 * v + 128 * h : 256 * v + 128 * (h + 1)]
            pack_ref[640 + 128 * h : 768 + 128 * h, 128 * v : 128 * (v + 1)] = rows
    for move in moves[6:]:
        move.wait()


def second_body(pack_ref, got_ref, one_ref, two_ref):
    first = (lax.axis_index("curve") & 1) == 0
    one = (pack_ref[256:384].astype(F32) + got_ref[256:384].astype(F32)).astype(BF16)
    one_ref[...] = one
    mine = pack_ref[896:1024]
    other = got_ref[896:1024]
    top = jnp.where(first, mine, other)
    bottom = jnp.where(first, other, mine)
    two_ref[...] = (nn(one[:, 0:128], top) + nn(one[:, 128:256], bottom)).astype(BF16)


def cross_body(pack_ref, got_ref, one_ref, out_ref):
    first = (lax.axis_index("curve") & 1) == 0
    out_ref[0:128] = jnp.where(first, pack_ref[0:128], got_ref[128:256])
    out_ref[128:256] = jnp.where(first, pack_ref[128:256], pack_ref[0:128])
    out_ref[256:384] = jnp.where(first, got_ref[0:128], pack_ref[128:256])
    out_ref[384:640] = jnp.where(first, pack_ref[640:896], pack_ref[384:640])
    out_ref[640:768] = one_ref[...]


def bundle_body(one_ref, cross_ref, out_ref):
    out_ref[0:128] = one_ref[...]
    out_ref[128:256] = cross_ref[640:768]


def couple_two_body(near_ref, far_ref, weights_ref, out_ref):
    first = weights_ref[:, 0].reshape(256, 256)
    second = weights_ref[:, 1].reshape(256, 256)
    value = (nn(near_ref[...], first) + nn(far_ref[...], second)).astype(BF16)
    for i in range(4):
        out_ref[i] = value


def gather_body(
    points,
    rank,
    table_ref,
    leaf_ref,
    got_ref,
    cross_ref,
    c0_hbm,
    self_hbm,
    next_hbm,
    x_hbm,
    mask_ref,
    zero_ref,
    weight_ref,
    field_ref,
    c0_ref,
    self_ref,
    next_ref,
    x_ref,
    sems,
):
    copies = [(x_hbm, x_ref)]
    for i in range(2):
        rows = pl.ds(i * points, points)
        copies.append((self_hbm.at[rows], self_ref.at[rows]))
        copies.append((next_hbm.at[rows], next_ref.at[rows]))
    copies.append((c0_hbm, c0_ref))
    moves = [pltpu.make_async_copy(a, b, sems.at[n]) for n, (a, b) in enumerate(copies)]
    for move in moves:
        move.start()
    device = lax.axis_index("curve")
    core = device & 1
    first = core == 0
    clusters = table_ref.shape[1]
    own = device // 2
    sign = jnp.where(first, -1, 1)
    row = picked_row(table_ref[...], own)
    for s in range(3):
        for n in range(2):
            mask = offset_mask(row[s : s + 1], own, (n + 2) * sign, clusters)
            mask_ref[2 * s + n : 2 * s + n + 1] = jnp.broadcast_to(mask, (1, 256))

    pieces = []
    ahead = []
    for h in range(2):
        pieces.append(
            jnp.where(
                first,
                cross_ref[384 + 128 * h : 512 + 128 * h],
                got_ref[384 + 128 * h : 512 + 128 * h],
            )
        )
        ahead.append(
            jnp.where(
                first,
                got_ref[640 + 128 * h : 768 + 128 * h],
                cross_ref[384 + 128 * h : 512 + 128 * h],
            )
        )
    incoming = jnp.concatenate(pieces, 1).astype(F32).T
    following = jnp.concatenate(
        [ahead[0][:, 0:128], ahead[1][:, 0:128], ahead[0][:, 128:256], ahead[1][:, 128:256]], 0
    )
    moves[0].wait()
    x0 = x_ref[0:points]
    x1 = x_ref[points : 2 * points]
    moves[1].wait()
    moves[2].wait()
    top = next_ref[0:points]
    field_ref[0:points] = nn(self_ref[0:points], x0) + nn(top, x1) + incoming
    inner = nn(x0.T, top).T
    moves[3].wait()
    moves[4].wait()
    field_ref[points : 2 * points] = (
        nn(self_ref[points : 2 * points], x1)
        + nn(next_ref[points : 2 * points], following)
        + inner
    )

    leaves = clusters * 4
    cross = [cross_ref[128 * n : 128 * (n + 1)].astype(F32) for n in range(3)]
    partner = [got_ref[128 * n : 128 * (n + 1)].astype(F32) for n in range(2)]

    def either(a, b):
        return jnp.where(first, a, b)

    nothing = jnp.zeros_like(cross[0])
    tables = (
        (
            (-3, either(cross[0], nothing)),
            (-2, either(cross[1], partner[0])),
            (2, either(partner[0], cross[0])),
            (3, either(partner[1], cross[1])),
        ),
        (
            (-3, either(cross[1], partner[0])),
            (-2, either(cross[2], partner[1])),
            (2, either(partner[1], cross[1])),
            (3, either(nothing, cross[2])),
        ),
    )
    moves[5].wait()
    weight = None
    for i in range(2):
        leaf = 2 * device + i
        total = None
        for s in range(3):
            entry = leaf_ref[i : i + 1, s : s + 1]
            chosen = None
            for offset, value in tables[i]:
                term = value * offset_mask(entry, leaf, offset, leaves)
                chosen = term if chosen is None else chosen + term
            block = c0_ref[s, i * rank : (i + 1) * rank]
            term = nn(chosen.astype(BF16), block)
            total = term if total is None else total + term
            edge = offset_mask(entry, leaf, 3 if i else -3, leaves)
            edge = edge * jnp.where(core == (1 - i), 1.0, 0.0)
            term = block.astype(F32) * edge
            weight = term if weight is None else weight + term
        zero_ref[128 * i : 128 * (i + 1)] = total
    weight_ref[...] = weight.astype(BF16)


def share_body(gathered_ref, near_ref, mask_ref, pack_ref, got_ref, cross_ref, out_ref):
    first = (lax.axis_index("curve") & 1) == 0
    near = near_ref[0:128].astype(F32)
    far = near_ref[128:256].astype(F32)
    one = None
    for s in range(3):
        chosen = near * mask_ref[2 * s : 2 * s + 1] + far * mask_ref[2 * s + 1 : 2 * s + 2]
        chosen = chosen.astype(BF16)
        mine = pack_ref[1024 + 128 * s : 1152 + 128 * s]
        other = got_ref[1024 + 128 * s : 1152 + 128 * s]
        term = nn(chosen[:, 0:128], jnp.where(first, mine, other))
        term = term + nn(chosen[:, 128:256], jnp.where(first, other, mine))
        one = term if one is None else one + term
    total = gathered_ref[0].astype(F32)
    for i in range(1, 4):
        total = total + gathered_ref[i].astype(F32)
    total = total.astype(BF16)
    mine = pack_ref[896:1024]
    other = got_ref[896:1024]
    top = nt(total, jnp.where(first, mine, other))
    bottom = nt(total, jnp.where(first, other, mine))
    out_ref[0:128] = (one + jnp.concatenate([top, bottom], 1)).astype(BF16)
    out_ref[128:256] = jnp.where(first, cross_ref[256:384], cross_ref[0:128])


def last_body(points, rank, mine_ref, got_ref, zero_ref, weight_ref, e1_ref, basis_ref, field_ref, out_ref):
    core = lax.axis_index("curve") & 1
    one = (mine_ref[0:128].astype(F32) + got_ref[0:128].astype(F32)).astype(BF16)
    extra = nn(got_ref[128:256], weight_ref[...])
    for i in range(2):
        used = jnp.where(core == (1 - i), 1.0, 0.0)
        zero = zero_ref[128 * i : 128 * (i + 1)] + extra * used
        zero = zero + nt(one, e1_ref[i * rank : (i + 1) * rank])
        field = nt(basis_ref[i * points : (i + 1) * points], zero.astype(BF16))
        out_ref[i * points : (i + 1) * points] = (
            field_ref[i * points : (i + 1) * points] + field
        ).astype(BF16)


def local_part(
    vectors,
    near_self,
    near_next,
    leaf_basis,
    transfer_one,
    transfer_two,
    coupling_zero,
    coupling_one,
    coupling_two,
    list_zero,
    list_one,
    list_two,
):
    size = lax.axis_size("curve")
    rank = leaf_basis.shape[1]
    points = near_self.shape[1]
    c0 = jnp.transpose(coupling_zero, (1, 0, 2))
    c1 = jnp.transpose(coupling_one, (1, 0, 2))
    c2 = jnp.transpose(coupling_two, (1, 0, 2))
    table_one = list_one.T
    table_two = list_two.T

    (spread,) = call(spread_body, [((8, 2, 32, 256), BF16)], 1 << 18, table_two, c2)
    weights_two = lax.all_to_all(
        spread, "curve", 0, 0, axis_index_groups=cluster_groups(size)
    )
    (pack,) = call(
        functools.partial(first_body, points, rank),
        [((1408, 256), BF16)],
        160 << 20,
        leaf_basis,
        vectors,
        transfer_one,
        near_next,
        transfer_two,
        c1,
        far=range(6),
        scratch=[
            pltpu.VMEM((2 * points, rank), BF16),
            pltpu.VMEM((2 * points, 128), BF16),
            pltpu.VMEM((2 * rank, rank), BF16),
            pltpu.VMEM((points, points), BF16),
            pltpu.SemaphoreType.DMA((10,)),
        ],
    )
    got = core_swap(pack)
    one, two = call(second_body, [((128, 256), BF16), ((128, 256), BF16)], 16 << 20, pack, got)
    two_far = third_cluster(two)
    two_near = far_route(two, 8)
    (leaves,) = call(cross_body, [((768, 256), BF16)], 1 << 18, pack, got, one)
    crossed = chip_swap(leaves)
    (coupled,) = call(
        couple_two_body, [((4, 128, 256), BF16)], 32 << 20, two_near, two_far, weights_two
    )
    gathered = lax.all_to_all(coupled, "curve", 0, 0, axis_index_groups=chip_groups(size))
    (bundle,) = call(bundle_body, [((256, 256), BF16)], 1 << 18, one, crossed)
    one_near = far_route(bundle, 2)
    mask, far_zero, weight, field = call(
        functools.partial(gather_body, points, rank),
        [
            ((8, 256), F32),
            ((256, 256), F32),
            ((256, 256), BF16),
            ((2 * points, 128), F32),
        ],
        500 << 20,
        table_one,
        list_zero,
        got,
        crossed,
        c0,
        near_self,
        near_next,
        vectors,
        far=range(4, 8),
        scratch=[
            pltpu.VMEM(c0.shape, BF16),
            pltpu.VMEM(near_self.shape, BF16),
            pltpu.VMEM(near_next.shape, BF16),
            pltpu.VMEM(vectors.shape, BF16),
            pltpu.SemaphoreType.DMA((6,)),
        ],
    )
    (share,) = call(
        share_body, [((256, 256), BF16)], 16 << 20, gathered, one_near, mask, pack, got, crossed
    )
    last = core_swap(share)
    (out,) = call(
        functools.partial(last_body, points, rank),
        [((2 * points, 128), BF16)],
        120 << 20,
        share,
        last,
        far_zero,
        weight,
        transfer_one,
        leaf_basis,
        field,
    )
    return out


def solution(mesh):
    rows = P("curve", None)
    cube = P("curve", None, None)
    return jax.shard_map(
        local_part,
        mesh=mesh,
        in_specs=(rows, rows, rows, rows, rows, rows, cube, cube, cube, rows, P(), P()),
        out_specs=rows,
        check_vma=False,
    )
```

```python
import functools

import jax
import jax.numpy as jnp
from jax import lax
from jax.experimental import pallas as pl
from jax.experimental.pallas import tpu as pltpu
from jax.sharding import PartitionSpec as P


F32 = jnp.float32
BF16 = jnp.bfloat16
I32 = jnp.int32


def route(value, source_of):
    size = lax.axis_size("curve")
    return lax.ppermute(value, "curve", [(source_of(i) % size, i) for i in range(size)])


def core_swap(value):
    return route(value, lambda i: i ^ 1)


def chip_swap(value):
    return route(value, lambda i: i + 1 if i & 1 else i - 1)


def far_route(value, chips):
    return route(value, lambda i: i + 2 * chips if i & 1 else i - 2 * chips)


def third_cluster(value):
    def source_of(i):
        turned = i ^ 4
        return turned + 24 if i & 1 else turned - 24

    return route(value, source_of)


def chip_groups(size):
    return [[8 * g + 2 * i + j for i in range(4)] for g in range(size // 8) for j in range(2)]


def cluster_groups(size):
    return [[8 * g + i for i in range(8)] for g in range(size // 8)]


def nn(a, b):
    return lax.dot_general(a, b, (((1,), (0,)), ((), ())), preferred_element_type=F32)


def nt(a, b):
    return lax.dot_general(a, b, (((1,), (1,)), ((), ())), preferred_element_type=F32)


def call(body, outs, flops, *args, far=(), far_out=(), scratch=(), grant=8):
    spec = pl.BlockSpec(memory_space=pltpu.VMEM)
    moved = sum(a.size * a.dtype.itemsize for a in args)
    args = [
        pltpu.with_memory_space_constraint(a, pltpu.HBM) if n in far else a
        for n, a in enumerate(args)
    ]
    hbm = pl.BlockSpec(memory_space=pltpu.HBM)
    return pl.pallas_call(
        body,
        out_shape=[jax.ShapeDtypeStruct(s, t) for s, t in outs],
        in_specs=[hbm if n in far else spec for n in range(len(args))],
        out_specs=[hbm if n in far_out else spec for n in range(len(outs))],
        scratch_shapes=list(scratch),
        compiler_params=pltpu.CompilerParams(vmem_limit_bytes=grant << 20),
        cost_estimate=pl.CostEstimate(flops=flops, bytes_accessed=moved, transcendentals=0),
    )(*args)


def picked_row(table, row):
    lanes = lax.broadcasted_iota(I32, table.shape, 1)
    return jnp.sum(jnp.where(lanes == row, table, 0), axis=1, keepdims=True)


def offset_mask(entry, own, offset, clusters):
    wanted = lax.rem(own + offset + clusters, clusters)
    return jnp.where(entry == wanted, 1.0, 0.0).astype(F32)


def first_body(
    points, rank, table_hbm, c2_hbm, basis_hbm, x_hbm, e1_hbm, next_hbm, e2_hbm, c1_hbm,
    pack_ref, spread_hbm,
    basis_ref, x_ref, e1_ref, next_ref, table_ref, c2_ref, spread_ref, sems, out_sems,
):
    copies = []
    for i in range(2):
        rows = pl.ds(i * points, points)
        copies.append((x_hbm.at[rows], x_ref.at[rows]))
        copies.append((basis_hbm.at[rows], basis_ref.at[rows]))
    copies.append((e1_hbm, e1_ref))
    copies.append((next_hbm.at[pl.ds(points, points)], next_ref))
    copies.append((e2_hbm, pack_ref.at[pl.ds(896, 128)]))
    for s in range(3):
        copies.append((c1_hbm.at[s], pack_ref.at[pl.ds(1024 + 128 * s, 128)]))
    copies.append((table_hbm, table_ref))
    copies.append((c2_hbm, c2_ref))
    moves = [pltpu.make_async_copy(a, b, sems.at[n]) for n, (a, b) in enumerate(copies)]
    for move in moves[-2:] + moves[:-2]:
        move.start()
    device = lax.axis_index("curve")
    clusters = table_ref.shape[1]
    own = device // 8
    for move in moves[-2:]:
        move.wait()
    row = picked_row(table_ref[...], own)
    for core, offsets in enumerate(((-2, -3), (2, 3))):
        for n, offset in enumerate(offsets):
            total = None
            for s in range(3):
                mask = offset_mask(row[s : s + 1], own, offset, clusters)
                term = c2_ref[s].astype(F32) * mask
                total = term if total is None else total + term
            spread_ref[core, n] = total.astype(BF16)
    sent = [
        pltpu.make_async_copy(spread_ref.at[m % 2], spread_hbm.at[m], out_sems.at[m])
        for m in range(8)
    ]
    for move in sent:
        move.start()
    coefs = []
    for i in range(2):
        moves[2 * i].wait()
        turned = x_ref[i * points : (i + 1) * points].T
        moves[2 * i + 1].wait()
        coef = nn(turned, basis_ref[i * points : (i + 1) * points]).astype(BF16)
        pack_ref[128 * i : 128 * (i + 1)] = coef
        coefs.append(coef)
    moves[4].wait()
    part = nn(coefs[0], e1_ref[0:rank]) + nn(coefs[1], e1_ref[rank : 2 * rank])
    pack_ref[256:384] = part.astype(BF16)
    moves[5].wait()
    outgoing = nn(turned, next_ref[...]).astype(BF16)
    for h in range(2):
        pack_ref[384 + 128 * h : 512 + 128 * h] = outgoing[:, 256 * h : 256 * (h + 1)]
        for v in range(2):
            rows = x_ref[256 * v + 128 * h : 256 * v + 128 * (h + 1)]
            pack_ref[640 + 128 * h : 768 + 128 * h, 128 * v : 128 * (v + 1)] = rows
    for move in moves[6:-2]:
        move.wait()
    for move in sent:
        move.wait()


def second_body(pack_ref, got_ref, one_ref, two_ref, out_ref):
    first = (lax.axis_index("curve") & 1) == 0
    one = (pack_ref[256:384].astype(F32) + got_ref[256:384].astype(F32)).astype(BF16)
    one_ref[...] = one
    mine = pack_ref[896:1024]
    other = got_ref[896:1024]
    top = jnp.where(first, mine, other)
    bottom = jnp.where(first, other, mine)
    two_ref[...] = (nn(one[:, 0:128], top) + nn(one[:, 128:256], bottom)).astype(BF16)
    out_ref[0:128] = jnp.where(first, pack_ref[0:128], got_ref[128:256])
    out_ref[128:256] = jnp.where(first, pack_ref[128:256], pack_ref[0:128])
    out_ref[256:384] = jnp.where(first, got_ref[0:128], pack_ref[128:256])
    out_ref[384:640] = jnp.where(first, pack_ref[640:896], pack_ref[384:640])


def bundle_body(one_ref, cross_ref, out_ref):
    out_ref[0:128] = one_ref[...]
    out_ref[128:256] = cross_ref[...]


def couple_two_body(near_ref, far_ref, weights_ref, out_hbm, value_ref, sems):
    first = weights_ref[:, 0].reshape(256, 256)
    second = weights_ref[:, 1].reshape(256, 256)
    value_ref[...] = (nn(near_ref[...], first) + nn(far_ref[...], second)).astype(BF16)
    moves = [pltpu.make_async_copy(value_ref, out_hbm.at[i], sems.at[i]) for i in range(4)]
    for move in moves:
        move.start()
    for move in moves:
        move.wait()


def gather_body(
    points,
    rank,
    table_ref,
    leaf_ref,
    got_ref,
    cross_ref,
    c0_hbm,
    self_hbm,
    next_hbm,
    x_hbm,
    mask_ref,
    zero_ref,
    weight_ref,
    field_ref,
    c0_ref,
    self_ref,
    next_ref,
    x_ref,
    sems,
):
    copies = [(x_hbm, x_ref)]
    for i in range(2):
        rows = pl.ds(i * points, points)
        copies.append((self_hbm.at[rows], self_ref.at[rows]))
        copies.append((next_hbm.at[rows], next_ref.at[rows]))
    copies.append((c0_hbm, c0_ref))
    moves = [pltpu.make_async_copy(a, b, sems.at[n]) for n, (a, b) in enumerate(copies)]
    for move in moves:
        move.start()
    device = lax.axis_index("curve")
    core = device & 1
    first = core == 0
    clusters = table_ref.shape[1]
    own = device // 2
    sign = jnp.where(first, -1, 1)
    row = picked_row(table_ref[...], own)
    for s in range(3):
        for n in range(2):
            mask = offset_mask(row[s : s + 1], own, (n + 2) * sign, clusters)
            mask_ref[2 * s + n : 2 * s + n + 1] = jnp.broadcast_to(mask, (1, 256))

    pieces = []
    ahead = []
    for h in range(2):
        pieces.append(
            jnp.where(
                first,
                cross_ref[384 + 128 * h : 512 + 128 * h],
                got_ref[384 + 128 * h : 512 + 128 * h],
            )
        )
        ahead.append(
            jnp.where(
                first,
                got_ref[640 + 128 * h : 768 + 128 * h],
                cross_ref[384 + 128 * h : 512 + 128 * h],
            )
        )
    incoming = jnp.concatenate(pieces, 1).astype(F32).T
    following = jnp.concatenate(
        [ahead[0][:, 0:128], ahead[1][:, 0:128], ahead[0][:, 128:256], ahead[1][:, 128:256]], 0
    )
    moves[0].wait()
    x0 = x_ref[0:points]
    x1 = x_ref[points : 2 * points]
    moves[1].wait()
    moves[2].wait()
    top = next_ref[0:points]
    field_ref[0:points] = nn(self_ref[0:points], x0) + nn(top, x1) + incoming
    inner = nn(x0.T, top).T
    moves[3].wait()
    moves[4].wait()
    field_ref[points : 2 * points] = (
        nn(self_ref[points : 2 * points], x1)
        + nn(next_ref[points : 2 * points], following)
        + inner
    )

    leaves = clusters * 4
    cross = [cross_ref[128 * n : 128 * (n + 1)].astype(F32) for n in range(3)]
    partner = [got_ref[128 * n : 128 * (n + 1)].astype(F32) for n in range(2)]

    def either(a, b):
        return jnp.where(first, a, b)

    nothing = jnp.zeros_like(cross[0])
    tables = (
        (
            (-3, either(cross[0], nothing)),
            (-2, either(cross[1], partner[0])),
            (2, either(partner[0], cross[0])),
            (3, either(partner[1], cross[1])),
        ),
        (
            (-3, either(cross[1], partner[0])),
            (-2, either(cross[2], partner[1])),
            (2, either(partner[1], cross[1])),
            (3, either(nothing, cross[2])),
        ),
    )
    moves[5].wait()
    weight = None
    for i in range(2):
        leaf = 2 * device + i
        total = None
        for s in range(3):
            entry = leaf_ref[i : i + 1, s : s + 1]
            chosen = None
            for offset, value in tables[i]:
                term = value * offset_mask(entry, leaf, offset, leaves)
                chosen = term if chosen is None else chosen + term
            block = c0_ref[s, i * rank : (i + 1) * rank]
            term = nn(chosen.astype(BF16), block)
            total = term if total is None else total + term
            edge = offset_mask(entry, leaf, 3 if i else -3, leaves)
            edge = edge * jnp.where(core == (1 - i), 1.0, 0.0)
            term = block.astype(F32) * edge
            weight = term if weight is None else weight + term
        zero_ref[128 * i : 128 * (i + 1)] = total
    weight_ref[...] = weight.astype(BF16)


def share_body(gathered_ref, near_ref, mask_ref, pack_ref, got_ref, cross_ref, out_ref):
    first = (lax.axis_index("curve") & 1) == 0
    near = near_ref[0:128].astype(F32)
    far = near_ref[128:256].astype(F32)
    one = None
    for s in range(3):
        chosen = near * mask_ref[2 * s : 2 * s + 1] + far * mask_ref[2 * s + 1 : 2 * s + 2]
        chosen = chosen.astype(BF16)
        mine = pack_ref[1024 + 128 * s : 1152 + 128 * s]
        other = got_ref[1024 + 128 * s : 1152 + 128 * s]
        term = nn(chosen[:, 0:128], jnp.where(first, mine, other))
        term = term + nn(chosen[:, 128:256], jnp.where(first, other, mine))
        one = term if one is None else one + term
    total = gathered_ref[0].astype(F32)
    for i in range(1, 4):
        total = total + gathered_ref[i].astype(F32)
    total = total.astype(BF16)
    mine = pack_ref[896:1024]
    other = got_ref[896:1024]
    top = nt(total, jnp.where(first, mine, other))
    bottom = nt(total, jnp.where(first, other, mine))
    out_ref[0:128] = (one + jnp.concatenate([top, bottom], 1)).astype(BF16)
    out_ref[128:256] = jnp.where(first, cross_ref[256:384], cross_ref[0:128])


def last_body(
    points, rank, mine_ref, got_ref, zero_ref, weight_ref, e1_ref, basis_ref, field_ref, out_hbm,
    out_ref, sems,
):
    core = lax.axis_index("curve") & 1
    one = (mine_ref[0:128].astype(F32) + got_ref[0:128].astype(F32)).astype(BF16)
    extra = nn(got_ref[128:256], weight_ref[...])
    moves = []
    for i in range(2):
        used = jnp.where(core == (1 - i), 1.0, 0.0)
        zero = zero_ref[128 * i : 128 * (i + 1)] + extra * used
        zero = zero + nt(one, e1_ref[i * rank : (i + 1) * rank])
        field = nt(basis_ref[i * points : (i + 1) * points], zero.astype(BF16))
        out_ref[i * points : (i + 1) * points] = (
            field_ref[i * points : (i + 1) * points] + field
        ).astype(BF16)
        rows = pl.ds(i * points, points)
        move = pltpu.make_async_copy(out_ref.at[rows], out_hbm.at[rows], sems.at[i])
        move.start()
        moves.append(move)
    for move in moves:
        move.wait()


def local_part(
    vectors,
    near_self,
    near_next,
    leaf_basis,
    transfer_one,
    transfer_two,
    coupling_zero,
    coupling_one,
    coupling_two,
    list_zero,
    list_one,
    list_two,
):
    size = lax.axis_size("curve")
    rank = leaf_basis.shape[1]
    points = near_self.shape[1]
    c0 = jnp.transpose(coupling_zero, (1, 0, 2))
    c1 = jnp.transpose(coupling_one, (1, 0, 2))
    c2 = jnp.transpose(coupling_two, (1, 0, 2))
    table_one = list_one.T
    table_two = list_two.T

    pack, spread = call(
        functools.partial(first_body, points, rank),
        [((1408, 256), BF16), ((8, 2, 32, 256), BF16)],
        160 << 20,
        table_two,
        c2,
        leaf_basis,
        vectors,
        transfer_one,
        near_next,
        transfer_two,
        c1,
        far=range(8),
        far_out=(1,),
        scratch=[
            pltpu.VMEM((2 * points, rank), BF16),
            pltpu.VMEM((2 * points, 128), BF16),
            pltpu.VMEM((2 * rank, rank), BF16),
            pltpu.VMEM((points, points), BF16),
            pltpu.VMEM(table_two.shape, I32),
            pltpu.VMEM(c2.shape, BF16),
            pltpu.VMEM((2, 2, 32, 256), BF16),
            pltpu.SemaphoreType.DMA((12,)),
            pltpu.SemaphoreType.DMA((8,)),
        ],
    )
    got = core_swap(pack)
    weights_two = lax.all_to_all(
        spread, "curve", 0, 0, axis_index_groups=cluster_groups(size)
    )
    one, two, leaves = call(
        second_body,
        [((128, 256), BF16), ((128, 256), BF16), ((640, 256), BF16)],
        16 << 20,
        pack,
        got,
    )
    two_far = third_cluster(two)
    two_near = far_route(two, 8)
    one_crossed = chip_swap(one)
    crossed = chip_swap(leaves)
    (coupled,) = call(
        couple_two_body,
        [((4, 128, 256), BF16)],
        32 << 20,
        two_near,
        two_far,
        weights_two,
        far_out=(0,),
        scratch=[pltpu.VMEM((128, 256), BF16), pltpu.SemaphoreType.DMA((4,))],
    )
    gathered = lax.all_to_all(coupled, "curve", 0, 0, axis_index_groups=chip_groups(size))
    (bundle,) = call(bundle_body, [((256, 256), BF16)], 1 << 18, one, one_crossed)
    one_near = far_route(bundle, 2)
    mask, far_zero, weight, field = call(
        functools.partial(gather_body, points, rank),
        [
            ((8, 256), F32),
            ((256, 256), F32),
            ((256, 256), BF16),
            ((2 * points, 128), F32),
        ],
        500 << 20,
        table_one,
        list_zero,
        got,
        crossed,
        c0,
        near_self,
        near_next,
        vectors,
        far=range(4, 8),
        scratch=[
            pltpu.VMEM(c0.shape, BF16),
            pltpu.VMEM(near_self.shape, BF16),
            pltpu.VMEM(near_next.shape, BF16),
            pltpu.VMEM(vectors.shape, BF16),
            pltpu.SemaphoreType.DMA((6,)),
        ],
    )
    (share,) = call(
        share_body, [((256, 256), BF16)], 16 << 20, gathered, one_near, mask, pack, got, crossed
    )
    last = core_swap(share)
    (out,) = call(
        functools.partial(last_body, points, rank),
        [((2 * points, 128), BF16)],
        120 << 20,
        share,
        last,
        far_zero,
        weight,
        transfer_one,
        leaf_basis,
        field,
        far_out=(0,),
        scratch=[pltpu.VMEM((2 * points, 128), BF16), pltpu.SemaphoreType.DMA((2,))],
    )
    return out


def solution(mesh):
    rows = P("curve", None)
    cube = P("curve", None, None)
    return jax.shard_map(
        local_part,
        mesh=mesh,
        in_specs=(rows, rows, rows, rows, rows, rows, cube, cube, cube, rows, P(), P()),
        out_specs=rows,
        check_vma=False,
    )
```

```python
import functools

import jax
import jax.numpy as jnp
from jax import lax
from jax.experimental import pallas as pl
from jax.experimental.pallas import tpu as pltpu
from jax.sharding import PartitionSpec as P


F32 = jnp.float32
BF16 = jnp.bfloat16
I32 = jnp.int32


def route(value, source_of):
    size = lax.axis_size("curve")
    return lax.ppermute(value, "curve", [(source_of(i) % size, i) for i in range(size)])


def core_swap(value):
    return route(value, lambda i: i ^ 1)


def chip_swap(value):
    return route(value, lambda i: i + 1 if i & 1 else i - 1)


def far_route(value, chips):
    return route(value, lambda i: i + 2 * chips if i & 1 else i - 2 * chips)


def third_cluster(value):
    def source_of(i):
        turned = i ^ 4
        return turned + 24 if i & 1 else turned - 24

    return route(value, source_of)


def chip_groups(size):
    return [[8 * g + 2 * i + j for i in range(4)] for g in range(size // 8) for j in range(2)]


def cluster_groups(size):
    return [[8 * g + i for i in range(8)] for g in range(size // 8)]


def nn(a, b):
    return lax.dot_general(a, b, (((1,), (0,)), ((), ())), preferred_element_type=F32)


def nt(a, b):
    return lax.dot_general(a, b, (((1,), (1,)), ((), ())), preferred_element_type=F32)


def call(body, outs, flops, *args, far=(), far_out=(), scratch=(), grant=8):
    spec = pl.BlockSpec(memory_space=pltpu.VMEM)
    moved = sum(a.size * a.dtype.itemsize for a in args)
    args = [
        pltpu.with_memory_space_constraint(a, pltpu.HBM) if n in far else a
        for n, a in enumerate(args)
    ]
    hbm = pl.BlockSpec(memory_space=pltpu.HBM)
    return pl.pallas_call(
        body,
        out_shape=[jax.ShapeDtypeStruct(s, t) for s, t in outs],
        in_specs=[hbm if n in far else spec for n in range(len(args))],
        out_specs=[hbm if n in far_out else spec for n in range(len(outs))],
        scratch_shapes=list(scratch),
        compiler_params=pltpu.CompilerParams(vmem_limit_bytes=grant << 20),
        cost_estimate=pl.CostEstimate(flops=flops, bytes_accessed=moved, transcendentals=0),
    )(*args)


def picked_row(table, row):
    lanes = lax.broadcasted_iota(I32, table.shape, 1)
    return jnp.sum(jnp.where(lanes == row, table, 0), axis=1, keepdims=True)


def offset_mask(entry, own, offset, clusters):
    wanted = lax.rem(own + offset + clusters, clusters)
    return jnp.where(entry == wanted, 1.0, 0.0).astype(F32)


def first_body(
    points, rank, table_hbm, c2_hbm, basis_hbm, x_hbm, e1_hbm, next_hbm, e2_hbm, c1_hbm,
    pack_ref, spread_hbm,
    basis_ref, x_ref, e1_ref, next_ref, table_ref, c2_ref, spread_ref, sems, out_sems,
):
    copies = []
    for i in range(2):
        rows = pl.ds(i * points, points)
        copies.append((x_hbm.at[rows], x_ref.at[rows]))
        copies.append((basis_hbm.at[rows], basis_ref.at[rows]))
    copies.append((e1_hbm, e1_ref))
    copies.append((next_hbm.at[pl.ds(points, points)], next_ref))
    copies.append((e2_hbm, pack_ref.at[pl.ds(896, 128)]))
    for s in range(3):
        copies.append((c1_hbm.at[s], pack_ref.at[pl.ds(1024 + 128 * s, 128)]))
    copies.append((table_hbm, table_ref))
    copies.append((c2_hbm, c2_ref))
    moves = [pltpu.make_async_copy(a, b, sems.at[n]) for n, (a, b) in enumerate(copies)]
    for move in moves[-2:] + moves[:-2]:
        move.start()
    device = lax.axis_index("curve")
    clusters = table_ref.shape[1]
    own = device // 8
    for move in moves[-2:]:
        move.wait()
    row = picked_row(table_ref[...], own)
    for core, offsets in enumerate(((-2, -3), (2, 3))):
        for n, offset in enumerate(offsets):
            total = None
            for s in range(3):
                mask = offset_mask(row[s : s + 1], own, offset, clusters)
                term = c2_ref[s].astype(F32) * mask
                total = term if total is None else total + term
            spread_ref[core, n] = total.astype(BF16)
    sent = [
        pltpu.make_async_copy(spread_ref.at[m % 2], spread_hbm.at[m], out_sems.at[m])
        for m in range(8)
    ]
    for move in sent:
        move.start()
    coefs = []
    for i in range(2):
        moves[2 * i].wait()
        turned = x_ref[i * points : (i + 1) * points].T
        moves[2 * i + 1].wait()
        coef = nn(turned, basis_ref[i * points : (i + 1) * points]).astype(BF16)
        pack_ref[128 * i : 128 * (i + 1)] = coef
        coefs.append(coef)
    moves[4].wait()
    part = nn(coefs[0], e1_ref[0:rank]) + nn(coefs[1], e1_ref[rank : 2 * rank])
    pack_ref[256:384] = part.astype(BF16)
    moves[5].wait()
    outgoing = nn(turned, next_ref[...]).astype(BF16)
    for h in range(2):
        pack_ref[384 + 128 * h : 512 + 128 * h] = outgoing[:, 256 * h : 256 * (h + 1)]
        for v in range(2):
            rows = x_ref[256 * v + 128 * h : 256 * v + 128 * (h + 1)]
            pack_ref[640 + 128 * h : 768 + 128 * h, 128 * v : 128 * (v + 1)] = rows
    for move in moves[6:-2]:
        move.wait()
    for move in sent:
        move.wait()


def second_body(pack_ref, got_ref, two_ref, edge_ref, out_ref):
    first = (lax.axis_index("curve") & 1) == 0
    one = (pack_ref[256:384].astype(F32) + got_ref[256:384].astype(F32)).astype(BF16)
    edge_ref[0:128] = one
    edge_ref[128:256] = jnp.where(first, pack_ref[0:128], pack_ref[128:256])
    mine = pack_ref[896:1024]
    other = got_ref[896:1024]
    top = jnp.where(first, mine, other)
    bottom = jnp.where(first, other, mine)
    two_ref[...] = (nn(one[:, 0:128], top) + nn(one[:, 128:256], bottom)).astype(BF16)
    out_ref[0:128] = jnp.where(first, pack_ref[128:256], got_ref[128:256])
    out_ref[128:256] = jnp.where(first, got_ref[0:128], pack_ref[0:128])
    out_ref[256:512] = jnp.where(first, pack_ref[640:896], pack_ref[384:640])


def bundle_body(edge_ref, crossed_ref, out_ref):
    out_ref[0:128] = edge_ref[0:128]
    out_ref[128:256] = crossed_ref[0:128]


def couple_two_body(near_ref, far_ref, weights_ref, out_hbm, value_ref, sems):
    first = weights_ref[:, 0].reshape(256, 256)
    second = weights_ref[:, 1].reshape(256, 256)
    value_ref[...] = (nn(near_ref[...], first) + nn(far_ref[...], second)).astype(BF16)
    moves = [pltpu.make_async_copy(value_ref, out_hbm.at[i], sems.at[i]) for i in range(4)]
    for move in moves:
        move.start()
    for move in moves:
        move.wait()


def near_body(
    points,
    rank,
    table_ref,
    leaf_ref,
    c0_hbm,
    self_hbm,
    next_hbm,
    x_hbm,
    mask_ref,
    weight_ref,
    field_ref,
    c0_ref,
    self_ref,
    next_ref,
    x_ref,
    sems,
):
    copies = [(x_hbm, x_ref)]
    for i in range(2):
        rows = pl.ds(i * points, points)
        copies.append((self_hbm.at[rows], self_ref.at[rows]))
    copies.append((next_hbm.at[pl.ds(0, points)], next_ref))
    copies.append((c0_hbm, c0_ref))
    moves = [pltpu.make_async_copy(a, b, sems.at[n]) for n, (a, b) in enumerate(copies)]
    for move in moves:
        move.start()
    device = lax.axis_index("curve")
    core = device & 1
    clusters = table_ref.shape[1]
    own = device // 2
    sign = jnp.where(core == 0, -1, 1)
    row = picked_row(table_ref[...], own)
    for s in range(3):
        for n in range(2):
            mask = offset_mask(row[s : s + 1], own, (n + 2) * sign, clusters)
            mask_ref[2 * s + n : 2 * s + n + 1] = jnp.broadcast_to(mask, (1, 256))
    moves[0].wait()
    x0 = x_ref[0:points]
    x1 = x_ref[points : 2 * points]
    moves[1].wait()
    moves[3].wait()
    top = next_ref[...]
    field_ref[0:points] = nn(self_ref[0:points], x0) + nn(top, x1)
    inner = nn(x0.T, top).T
    moves[2].wait()
    field_ref[points : 2 * points] = nn(self_ref[points : 2 * points], x1) + inner
    leaves = clusters * 4
    moves[4].wait()
    weight = None
    for i in range(2):
        leaf = 2 * device + i
        for s in range(3):
            entry = leaf_ref[i : i + 1, s : s + 1]
            edge = offset_mask(entry, leaf, 3 if i else -3, leaves)
            edge = edge * jnp.where(core == (1 - i), 1.0, 0.0)
            term = c0_ref[s, i * rank : (i + 1) * rank].astype(F32) * edge
            weight = term if weight is None else weight + term
    weight_ref[...] = weight.astype(BF16)


def gather_body(
    points,
    rank,
    leaf_ref,
    got_ref,
    edge_ref,
    cross_ref,
    c0_ref,
    next_ref,
    part_ref,
    zero_ref,
    field_ref,
):
    device = lax.axis_index("curve")
    first = (device & 1) == 0
    leaves = 2 * lax.axis_size("curve")

    def either(a, b):
        return jnp.where(first, a, b)

    pieces = []
    ahead = []
    for h in range(2):
        crossed = cross_ref[256 + 128 * h : 384 + 128 * h]
        pieces.append(either(crossed, got_ref[384 + 128 * h : 512 + 128 * h]))
        ahead.append(either(got_ref[640 + 128 * h : 768 + 128 * h], crossed))
    incoming = jnp.concatenate(pieces, 1).astype(F32).T
    following = jnp.concatenate(
        [ahead[0][:, 0:128], ahead[1][:, 0:128], ahead[0][:, 128:256], ahead[1][:, 128:256]], 0
    )
    field_ref[0:points] = part_ref[0:points] + incoming
    field_ref[points : 2 * points] = part_ref[points : 2 * points] + nn(
        next_ref[points : 2 * points], following
    )
    edge = edge_ref[128:256].astype(F32)
    rest = [cross_ref[128 * n : 128 * (n + 1)].astype(F32) for n in range(2)]
    partner = [got_ref[128 * n : 128 * (n + 1)].astype(F32) for n in range(2)]
    cross = (either(rest[0], edge), either(rest[1], rest[0]), either(edge, rest[1]))
    nothing = jnp.zeros_like(edge)
    tables = (
        (
            (-3, either(cross[0], nothing)),
            (-2, either(cross[1], partner[0])),
            (2, either(partner[0], cross[0])),
            (3, either(partner[1], cross[1])),
        ),
        (
            (-3, either(cross[1], partner[0])),
            (-2, either(cross[2], partner[1])),
            (2, either(partner[1], cross[1])),
            (3, either(nothing, cross[2])),
        ),
    )
    for i in range(2):
        leaf = 2 * device + i
        total = None
        for s in range(3):
            entry = leaf_ref[i : i + 1, s : s + 1]
            chosen = None
            for offset, value in tables[i]:
                term = value * offset_mask(entry, leaf, offset, leaves)
                chosen = term if chosen is None else chosen + term
            term = nn(chosen.astype(BF16), c0_ref[s, i * rank : (i + 1) * rank])
            total = term if total is None else total + term
        zero_ref[128 * i : 128 * (i + 1)] = total


def share_body(gathered_ref, near_ref, mask_ref, pack_ref, got_ref, edge_ref, out_ref):
    first = (lax.axis_index("curve") & 1) == 0
    near = near_ref[0:128].astype(F32)
    far = near_ref[128:256].astype(F32)
    one = None
    for s in range(3):
        chosen = near * mask_ref[2 * s : 2 * s + 1] + far * mask_ref[2 * s + 1 : 2 * s + 2]
        chosen = chosen.astype(BF16)
        mine = pack_ref[1024 + 128 * s : 1152 + 128 * s]
        other = got_ref[1024 + 128 * s : 1152 + 128 * s]
        term = nn(chosen[:, 0:128], jnp.where(first, mine, other))
        term = term + nn(chosen[:, 128:256], jnp.where(first, other, mine))
        one = term if one is None else one + term
    total = gathered_ref[0].astype(F32)
    for i in range(1, 4):
        total = total + gathered_ref[i].astype(F32)
    total = total.astype(BF16)
    mine = pack_ref[896:1024]
    other = got_ref[896:1024]
    top = nt(total, jnp.where(first, mine, other))
    bottom = nt(total, jnp.where(first, other, mine))
    out_ref[0:128] = (one + jnp.concatenate([top, bottom], 1)).astype(BF16)
    out_ref[128:256] = edge_ref[128:256]


def last_body(
    points, rank, mine_ref, got_ref, zero_ref, weight_ref, e1_ref, basis_ref, field_ref, out_hbm,
    out_ref, sems,
):
    core = lax.axis_index("curve") & 1
    one = (mine_ref[0:128].astype(F32) + got_ref[0:128].astype(F32)).astype(BF16)
    extra = nn(got_ref[128:256], weight_ref[...])
    moves = []
    for i in range(2):
        used = jnp.where(core == (1 - i), 1.0, 0.0)
        zero = zero_ref[128 * i : 128 * (i + 1)] + extra * used
        zero = zero + nt(one, e1_ref[i * rank : (i + 1) * rank])
        field = nt(basis_ref[i * points : (i + 1) * points], zero.astype(BF16))
        out_ref[i * points : (i + 1) * points] = (
            field_ref[i * points : (i + 1) * points] + field
        ).astype(BF16)
        rows = pl.ds(i * points, points)
        move = pltpu.make_async_copy(out_ref.at[rows], out_hbm.at[rows], sems.at[i])
        move.start()
        moves.append(move)
    for move in moves:
        move.wait()


def local_part(
    vectors,
    near_self,
    near_next,
    leaf_basis,
    transfer_one,
    transfer_two,
    coupling_zero,
    coupling_one,
    coupling_two,
    list_zero,
    list_one,
    list_two,
):
    size = lax.axis_size("curve")
    rank = leaf_basis.shape[1]
    points = near_self.shape[1]
    c0 = jnp.transpose(coupling_zero, (1, 0, 2))
    c1 = jnp.transpose(coupling_one, (1, 0, 2))
    c2 = jnp.transpose(coupling_two, (1, 0, 2))
    table_one = list_one.T
    table_two = list_two.T

    pack, spread = call(
        functools.partial(first_body, points, rank),
        [((1408, 256), BF16), ((8, 2, 32, 256), BF16)],
        160 << 20,
        table_two,
        c2,
        leaf_basis,
        vectors,
        transfer_one,
        near_next,
        transfer_two,
        c1,
        far=range(8),
        far_out=(1,),
        scratch=[
            pltpu.VMEM((2 * points, rank), BF16),
            pltpu.VMEM((2 * points, 128), BF16),
            pltpu.VMEM((2 * rank, rank), BF16),
            pltpu.VMEM((points, points), BF16),
            pltpu.VMEM(table_two.shape, I32),
            pltpu.VMEM(c2.shape, BF16),
            pltpu.VMEM((2, 2, 32, 256), BF16),
            pltpu.SemaphoreType.DMA((12,)),
            pltpu.SemaphoreType.DMA((8,)),
        ],
    )
    got = core_swap(pack)
    weights_two = lax.all_to_all(
        spread, "curve", 0, 0, axis_index_groups=cluster_groups(size)
    )
    two, edge, leaves = call(
        second_body,
        [((128, 256), BF16), ((256, 256), BF16), ((512, 256), BF16)],
        16 << 20,
        pack,
        got,
    )
    two_far = third_cluster(two)
    two_near = far_route(two, 8)
    edge_crossed = chip_swap(edge)
    crossed = chip_swap(leaves)
    (coupled,) = call(
        couple_two_body,
        [((4, 128, 256), BF16)],
        32 << 20,
        two_near,
        two_far,
        weights_two,
        far_out=(0,),
        scratch=[pltpu.VMEM((128, 256), BF16), pltpu.SemaphoreType.DMA((4,))],
    )
    gathered = lax.all_to_all(coupled, "curve", 0, 0, axis_index_groups=chip_groups(size))
    (bundle,) = call(bundle_body, [((256, 256), BF16)], 1 << 18, edge, edge_crossed)
    one_near = far_route(bundle, 2)
    mask, weight, part = call(
        functools.partial(near_body, points, rank),
        [((8, 256), F32), ((256, 256), BF16), ((2 * points, 128), F32)],
        300 << 20,
        table_one,
        list_zero,
        c0,
        near_self,
        near_next,
        vectors,
        far=range(2, 6),
        scratch=[
            pltpu.VMEM(c0.shape, BF16),
            pltpu.VMEM(near_self.shape, BF16),
            pltpu.VMEM((points, points), BF16),
            pltpu.VMEM(vectors.shape, BF16),
            pltpu.SemaphoreType.DMA((5,)),
        ],
    )
    (share,) = call(
        share_body,
        [((256, 256), BF16)],
        16 << 20,
        gathered,
        one_near,
        mask,
        pack,
        got,
        edge_crossed,
    )
    last = core_swap(share)
    far_zero, field = call(
        functools.partial(gather_body, points, rank),
        [((256, 256), F32), ((2 * points, 128), F32)],
        150 << 20,
        list_zero,
        got,
        edge_crossed,
        crossed,
        c0,
        near_next,
        part,
    )
    (out,) = call(
        functools.partial(last_body, points, rank),
        [((2 * points, 128), BF16)],
        120 << 20,
        share,
        last,
        far_zero,
        weight,
        transfer_one,
        leaf_basis,
        field,
        far_out=(0,),
        scratch=[pltpu.VMEM((2 * points, 128), BF16), pltpu.SemaphoreType.DMA((2,))],
    )
    return out


def solution(mesh):
    rows = P("curve", None)
    cube = P("curve", None, None)
    return jax.shard_map(
        local_part,
        mesh=mesh,
        in_specs=(rows, rows, rows, rows, rows, rows, cube, cube, cube, rows, P(), P()),
        out_specs=rows,
        check_vma=False,
    )
```

```python
import functools

import jax
import jax.numpy as jnp
from jax import lax
from jax.experimental import pallas as pl
from jax.experimental.pallas import tpu as pltpu
from jax.sharding import PartitionSpec as P


F32 = jnp.float32
BF16 = jnp.bfloat16
I32 = jnp.int32


def route(value, source_of):
    size = lax.axis_size("curve")
    return lax.ppermute(value, "curve", [(source_of(i) % size, i) for i in range(size)])


def core_swap(value):
    return route(value, lambda i: i ^ 1)


def chip_swap(value):
    return route(value, lambda i: i + 1 if i & 1 else i - 1)


def far_route(value, chips):
    return route(value, lambda i: i + 2 * chips if i & 1 else i - 2 * chips)


def third_cluster(value):
    def source_of(i):
        turned = i ^ 4
        return turned + 24 if i & 1 else turned - 24

    return route(value, source_of)


def chip_groups(size):
    return [[8 * g + 2 * i + j for i in range(4)] for g in range(size // 8) for j in range(2)]


def cluster_groups(size):
    return [[8 * g + i for i in range(8)] for g in range(size // 8)]


def nn(a, b):
    return lax.dot_general(a, b, (((1,), (0,)), ((), ())), preferred_element_type=F32)


def nt(a, b):
    return lax.dot_general(a, b, (((1,), (1,)), ((), ())), preferred_element_type=F32)


def call(body, outs, flops, *args, far=(), far_out=(), scratch=(), grant=8):
    spec = pl.BlockSpec(memory_space=pltpu.VMEM)
    moved = sum(a.size * a.dtype.itemsize for a in args)
    args = [
        pltpu.with_memory_space_constraint(a, pltpu.HBM) if n in far else a
        for n, a in enumerate(args)
    ]
    hbm = pl.BlockSpec(memory_space=pltpu.HBM)
    return pl.pallas_call(
        body,
        out_shape=[jax.ShapeDtypeStruct(s, t) for s, t in outs],
        in_specs=[hbm if n in far else spec for n in range(len(args))],
        out_specs=[hbm if n in far_out else spec for n in range(len(outs))],
        scratch_shapes=list(scratch),
        compiler_params=pltpu.CompilerParams(vmem_limit_bytes=grant << 20),
        cost_estimate=pl.CostEstimate(flops=flops, bytes_accessed=moved, transcendentals=0),
    )(*args)


def picked_row(table, row):
    lanes = lax.broadcasted_iota(I32, table.shape, 1)
    return jnp.sum(jnp.where(lanes == row, table, 0), axis=1, keepdims=True)


def offset_mask(entry, own, offset, clusters):
    wanted = lax.rem(own + offset + clusters, clusters)
    return jnp.where(entry == wanted, 1.0, 0.0).astype(F32)


def first_body(
    points, rank, table_hbm, c2_hbm, basis_hbm, x_hbm, e1_hbm, next_hbm, e2_hbm, c1_hbm,
    pack_ref, spread_hbm,
    basis_ref, x_ref, e1_ref, next_ref, table_ref, c2_ref, spread_ref, sems, out_sems,
):
    copies = []
    for i in range(2):
        rows = pl.ds(i * points, points)
        copies.append((x_hbm.at[rows], x_ref.at[rows]))
        copies.append((basis_hbm.at[rows], basis_ref.at[rows]))
    copies.append((e1_hbm, e1_ref))
    copies.append((next_hbm.at[pl.ds(points, points)], next_ref))
    copies.append((e2_hbm, pack_ref.at[pl.ds(896, 128)]))
    for s in range(3):
        copies.append((c1_hbm.at[s], pack_ref.at[pl.ds(1024 + 128 * s, 128)]))
    copies.append((table_hbm, table_ref))
    copies.append((c2_hbm, c2_ref))
    moves = [pltpu.make_async_copy(a, b, sems.at[n]) for n, (a, b) in enumerate(copies)]
    for move in moves[-2:] + moves[:-2]:
        move.start()
    device = lax.axis_index("curve")
    clusters = table_ref.shape[1]
    own = device // 8
    for move in moves[-2:]:
        move.wait()
    row = picked_row(table_ref[...], own)
    for core, offsets in enumerate(((-2, -3), (2, 3))):
        for n, offset in enumerate(offsets):
            total = None
            for s in range(3):
                mask = offset_mask(row[s : s + 1], own, offset, clusters)
                term = c2_ref[s].astype(F32) * mask
                total = term if total is None else total + term
            spread_ref[core, n] = total.astype(BF16)
    sent = [
        pltpu.make_async_copy(spread_ref.at[m % 2], spread_hbm.at[m], out_sems.at[m])
        for m in range(8)
    ]
    for move in sent:
        move.start()
    coefs = []
    for i in range(2):
        moves[2 * i].wait()
        turned = x_ref[i * points : (i + 1) * points].T
        moves[2 * i + 1].wait()
        coef = nn(turned, basis_ref[i * points : (i + 1) * points]).astype(BF16)
        pack_ref[128 * i : 128 * (i + 1)] = coef
        coefs.append(coef)
    moves[4].wait()
    part = nn(coefs[0], e1_ref[0:rank]) + nn(coefs[1], e1_ref[rank : 2 * rank])
    pack_ref[256:384] = part.astype(BF16)
    moves[5].wait()
    outgoing = nn(turned, next_ref[...]).astype(BF16)
    for h in range(2):
        pack_ref[384 + 128 * h : 512 + 128 * h] = outgoing[:, 256 * h : 256 * (h + 1)]
        for v in range(2):
            rows = x_ref[256 * v + 128 * h : 256 * v + 128 * (h + 1)]
            pack_ref[640 + 128 * h : 768 + 128 * h, 128 * v : 128 * (v + 1)] = rows
    for move in moves[6:-2]:
        move.wait()
    for move in sent:
        move.wait()


def second_body(pack_ref, got_ref, two_ref, edge_ref, out_ref):
    first = (lax.axis_index("curve") & 1) == 0
    one = (pack_ref[256:384].astype(F32) + got_ref[256:384].astype(F32)).astype(BF16)
    edge_ref[0:128] = one
    edge_ref[128:256] = jnp.where(first, pack_ref[0:128], pack_ref[128:256])
    mine = pack_ref[896:1024]
    other = got_ref[896:1024]
    top = jnp.where(first, mine, other)
    bottom = jnp.where(first, other, mine)
    two_ref[...] = (nn(one[:, 0:128], top) + nn(one[:, 128:256], bottom)).astype(BF16)
    out_ref[0:128] = jnp.where(first, pack_ref[128:256], got_ref[128:256])
    out_ref[128:256] = jnp.where(first, got_ref[0:128], pack_ref[0:128])
    out_ref[256:512] = jnp.where(first, pack_ref[640:896], pack_ref[384:640])


def bundle_body(edge_ref, crossed_ref, out_ref):
    out_ref[0:128] = edge_ref[0:128]
    out_ref[128:256] = crossed_ref[0:128]


def couple_two_body(near_ref, far_ref, weights_ref, out_hbm, value_ref, sems):
    first = weights_ref[:, 0].reshape(256, 256)
    second = weights_ref[:, 1].reshape(256, 256)
    value_ref[...] = (nn(near_ref[...], first) + nn(far_ref[...], second)).astype(BF16)
    moves = [pltpu.make_async_copy(value_ref, out_hbm.at[i], sems.at[i]) for i in range(4)]
    for move in moves:
        move.start()
    for move in moves:
        move.wait()


def near_body(
    points,
    rank,
    table_hbm,
    leaf_hbm,
    c0_hbm,
    self_hbm,
    next_hbm,
    x_hbm,
    mask_ref,
    weight_ref,
    field_ref,
    leaf_ref,
    table_ref,
    c0_ref,
    self_ref,
    next_ref,
    x_ref,
    sems,
):
    copies = [(x_hbm, x_ref)]
    for i in range(2):
        rows = pl.ds(i * points, points)
        copies.append((self_hbm.at[rows], self_ref.at[rows]))
    copies.append((next_hbm.at[pl.ds(0, points)], next_ref))
    copies.append((c0_hbm, c0_ref))
    copies.append((table_hbm, table_ref))
    copies.append((leaf_hbm, leaf_ref))
    moves = [pltpu.make_async_copy(a, b, sems.at[n]) for n, (a, b) in enumerate(copies)]
    for move in moves[-2:] + moves[:-2]:
        move.start()
    device = lax.axis_index("curve")
    core = device & 1
    clusters = table_ref.shape[1]
    own = device // 2
    moves[5].wait()
    moves[6].wait()
    sign = jnp.where(core == 0, -1, 1)
    row = picked_row(table_ref[...], own)
    for s in range(3):
        for n in range(2):
            mask = offset_mask(row[s : s + 1], own, (n + 2) * sign, clusters)
            mask_ref[2 * s + n : 2 * s + n + 1] = jnp.broadcast_to(mask, (1, 256))
    moves[0].wait()
    x0 = x_ref[0:points]
    x1 = x_ref[points : 2 * points]
    moves[1].wait()
    moves[3].wait()
    top = next_ref[...]
    field_ref[0:points] = nn(self_ref[0:points], x0) + nn(top, x1)
    inner = nn(x0.T, top).T
    moves[2].wait()
    field_ref[points : 2 * points] = nn(self_ref[points : 2 * points], x1) + inner
    leaves = clusters * 4
    moves[4].wait()
    weight = None
    for i in range(2):
        leaf = 2 * device + i
        for s in range(3):
            entry = leaf_ref[i : i + 1, s : s + 1]
            edge = offset_mask(entry, leaf, 3 if i else -3, leaves)
            edge = edge * jnp.where(core == (1 - i), 1.0, 0.0)
            term = c0_ref[s, i * rank : (i + 1) * rank].astype(F32) * edge
            weight = term if weight is None else weight + term
    weight_ref[...] = weight.astype(BF16)


def gather_body(
    points,
    rank,
    leaf_ref,
    got_ref,
    edge_ref,
    cross_ref,
    c0_ref,
    next_ref,
    part_ref,
    zero_ref,
    field_ref,
):
    device = lax.axis_index("curve")
    first = (device & 1) == 0
    leaves = 2 * lax.axis_size("curve")

    def either(a, b):
        return jnp.where(first, a, b)

    pieces = []
    ahead = []
    for h in range(2):
        crossed = cross_ref[256 + 128 * h : 384 + 128 * h]
        pieces.append(either(crossed, got_ref[384 + 128 * h : 512 + 128 * h]))
        ahead.append(either(got_ref[640 + 128 * h : 768 + 128 * h], crossed))
    incoming = jnp.concatenate(pieces, 1).astype(F32).T
    following = jnp.concatenate(
        [ahead[0][:, 0:128], ahead[1][:, 0:128], ahead[0][:, 128:256], ahead[1][:, 128:256]], 0
    )
    field_ref[0:points] = part_ref[0:points] + incoming
    field_ref[points : 2 * points] = part_ref[points : 2 * points] + nn(
        next_ref[points : 2 * points], following
    )
    edge = edge_ref[128:256].astype(F32)
    rest = [cross_ref[128 * n : 128 * (n + 1)].astype(F32) for n in range(2)]
    partner = [got_ref[128 * n : 128 * (n + 1)].astype(F32) for n in range(2)]
    cross = (either(rest[0], edge), either(rest[1], rest[0]), either(edge, rest[1]))
    nothing = jnp.zeros_like(edge)
    tables = (
        (
            (-3, either(cross[0], nothing)),
            (-2, either(cross[1], partner[0])),
            (2, either(partner[0], cross[0])),
            (3, either(partner[1], cross[1])),
        ),
        (
            (-3, either(cross[1], partner[0])),
            (-2, either(cross[2], partner[1])),
            (2, either(partner[1], cross[1])),
            (3, either(nothing, cross[2])),
        ),
    )
    for i in range(2):
        leaf = 2 * device + i
        total = None
        for s in range(3):
            entry = leaf_ref[i : i + 1, s : s + 1]
            chosen = None
            for offset, value in tables[i]:
                term = value * offset_mask(entry, leaf, offset, leaves)
                chosen = term if chosen is None else chosen + term
            term = nn(chosen.astype(BF16), c0_ref[s, i * rank : (i + 1) * rank])
            total = term if total is None else total + term
        zero_ref[128 * i : 128 * (i + 1)] = total


def share_body(gathered_ref, near_ref, mask_ref, pack_ref, got_ref, edge_ref, out_ref):
    first = (lax.axis_index("curve") & 1) == 0
    near = near_ref[0:128].astype(F32)
    far = near_ref[128:256].astype(F32)
    one = None
    for s in range(3):
        chosen = near * mask_ref[2 * s : 2 * s + 1] + far * mask_ref[2 * s + 1 : 2 * s + 2]
        chosen = chosen.astype(BF16)
        mine = pack_ref[1024 + 128 * s : 1152 + 128 * s]
        other = got_ref[1024 + 128 * s : 1152 + 128 * s]
        term = nn(chosen[:, 0:128], jnp.where(first, mine, other))
        term = term + nn(chosen[:, 128:256], jnp.where(first, other, mine))
        one = term if one is None else one + term
    total = gathered_ref[0].astype(F32)
    for i in range(1, 4):
        total = total + gathered_ref[i].astype(F32)
    total = total.astype(BF16)
    mine = pack_ref[896:1024]
    other = got_ref[896:1024]
    top = nt(total, jnp.where(first, mine, other))
    bottom = nt(total, jnp.where(first, other, mine))
    out_ref[0:128] = (one + jnp.concatenate([top, bottom], 1)).astype(BF16)
    out_ref[128:256] = edge_ref[128:256]


def last_body(
    points, rank, mine_ref, got_ref, zero_ref, weight_ref, e1_ref, basis_ref, field_ref, out_hbm,
    out_ref, sems,
):
    core = lax.axis_index("curve") & 1
    one = (mine_ref[0:128].astype(F32) + got_ref[0:128].astype(F32)).astype(BF16)
    extra = nn(got_ref[128:256], weight_ref[...])
    moves = []
    for i in range(2):
        used = jnp.where(core == (1 - i), 1.0, 0.0)
        zero = zero_ref[128 * i : 128 * (i + 1)] + extra * used
        zero = zero + nt(one, e1_ref[i * rank : (i + 1) * rank])
        field = nt(basis_ref[i * points : (i + 1) * points], zero.astype(BF16))
        out_ref[i * points : (i + 1) * points] = (
            field_ref[i * points : (i + 1) * points] + field
        ).astype(BF16)
        rows = pl.ds(i * points, points)
        move = pltpu.make_async_copy(out_ref.at[rows], out_hbm.at[rows], sems.at[i])
        move.start()
        moves.append(move)
    for move in moves:
        move.wait()


def local_part(
    vectors,
    near_self,
    near_next,
    leaf_basis,
    transfer_one,
    transfer_two,
    coupling_zero,
    coupling_one,
    coupling_two,
    list_zero,
    list_one,
    list_two,
):
    size = lax.axis_size("curve")
    rank = leaf_basis.shape[1]
    points = near_self.shape[1]
    c0 = jnp.transpose(coupling_zero, (1, 0, 2))
    c1 = jnp.transpose(coupling_one, (1, 0, 2))
    c2 = jnp.transpose(coupling_two, (1, 0, 2))
    table_one = list_one.T
    table_two = list_two.T

    pack, spread = call(
        functools.partial(first_body, points, rank),
        [((1408, 256), BF16), ((8, 2, 32, 256), BF16)],
        160 << 20,
        table_two,
        c2,
        leaf_basis,
        vectors,
        transfer_one,
        near_next,
        transfer_two,
        c1,
        far=range(8),
        far_out=(1,),
        scratch=[
            pltpu.VMEM((2 * points, rank), BF16),
            pltpu.VMEM((2 * points, 128), BF16),
            pltpu.VMEM((2 * rank, rank), BF16),
            pltpu.VMEM((points, points), BF16),
            pltpu.VMEM(table_two.shape, I32),
            pltpu.VMEM(c2.shape, BF16),
            pltpu.VMEM((2, 2, 32, 256), BF16),
            pltpu.SemaphoreType.DMA((12,)),
            pltpu.SemaphoreType.DMA((8,)),
        ],
    )
    got = core_swap(pack)
    weights_two = lax.all_to_all(
        spread, "curve", 0, 0, axis_index_groups=cluster_groups(size)
    )
    two, edge, leaves = call(
        second_body,
        [((128, 256), BF16), ((256, 256), BF16), ((512, 256), BF16)],
        16 << 20,
        pack,
        got,
    )
    two_far = third_cluster(two)
    two_near = far_route(two, 8)
    edge_crossed = chip_swap(edge)
    crossed = chip_swap(leaves)
    (coupled,) = call(
        couple_two_body,
        [((4, 128, 256), BF16)],
        32 << 20,
        two_near,
        two_far,
        weights_two,
        far_out=(0,),
        scratch=[pltpu.VMEM((128, 256), BF16), pltpu.SemaphoreType.DMA((4,))],
    )
    gathered = lax.all_to_all(coupled, "curve", 0, 0, axis_index_groups=chip_groups(size))
    (bundle,) = call(bundle_body, [((256, 256), BF16)], 1 << 18, edge, edge_crossed)
    one_near = far_route(bundle, 2)
    mask, weight, part, leaf_list = call(
        functools.partial(near_body, points, rank),
        [((8, 256), F32), ((256, 256), BF16), ((2 * points, 128), F32), (list_zero.shape, I32)],
        300 << 20,
        table_one,
        list_zero,
        c0,
        near_self,
        near_next,
        vectors,
        far=range(6),
        scratch=[
            pltpu.VMEM(table_one.shape, I32),
            pltpu.VMEM(c0.shape, BF16),
            pltpu.VMEM(near_self.shape, BF16),
            pltpu.VMEM((points, points), BF16),
            pltpu.VMEM(vectors.shape, BF16),
            pltpu.SemaphoreType.DMA((7,)),
        ],
    )
    (share,) = call(
        share_body,
        [((256, 256), BF16)],
        16 << 20,
        gathered,
        one_near,
        mask,
        pack,
        got,
        edge_crossed,
    )
    last = core_swap(share)
    far_zero, field = call(
        functools.partial(gather_body, points, rank),
        [((256, 256), F32), ((2 * points, 128), F32)],
        150 << 20,
        leaf_list,
        got,
        edge_crossed,
        crossed,
        c0,
        near_next,
        part,
    )
    (out,) = call(
        functools.partial(last_body, points, rank),
        [((2 * points, 128), BF16)],
        120 << 20,
        share,
        last,
        far_zero,
        weight,
        transfer_one,
        leaf_basis,
        field,
        far_out=(0,),
        scratch=[pltpu.VMEM((2 * points, 128), BF16), pltpu.SemaphoreType.DMA((2,))],
    )
    return out


def solution(mesh):
    rows = P("curve", None)
    cube = P("curve", None, None)
    return jax.shard_map(
        local_part,
        mesh=mesh,
        in_specs=(rows, rows, rows, rows, rows, rows, cube, cube, cube, rows, P(), P()),
        out_specs=rows,
        check_vma=False,
    )
```
